512 devices in a mesh: tm: 8 (over z), lat: 8 (over y_lo, core), lon: 8 (over x, y_hi).
Axes of the slice: x: 4, y: 8 (y_hi: 2, y_lo: 4; y = y_hi * 4 + y_lo), z: 8, core: 2. Of those that a mesh axis runs over, the one named last changes fastest.
Arguments:
- depth_class: int32 [1088, 3072], P('lat', 'lon'), may hold values from 0 to 31
- ocean_mask: int32 [1088, 3072], P('lat', 'lon'), may hold values 0 or 1
- depth_levels: float32 [32], replicated, may hold values from 0.1 to 1
- drag: float32 [1088, 3072], P('lat', 'lon'), may hold values from 0.0005 to 0.02
- tide_force: float32 [2, 1088, 3072], P(None, 'lat', 'lon'), may hold values from -6 to 6
- forward_flow: float32 [4, 1088, 3072], P(None, 'lat', 'lon'), may hold values from -6 to 6
- guess: float32 [8, 3, 1088, 3072], P('tm', None, 'lat', 'lon'), may hold values from -4 to 4
Outputs:
- final_state: float32 [8, 3, 1088, 3072], P('tm', None, 'lat', 'lon')
- drag_gradient: float32 [1088, 3072], P('lat', 'lon')
The draws below stay inside these ranges and needn't reach their ends.
Inputs may be any that keep to these rules, and one draw needn't show every extreme that they name: `depth_class`: index into depth_levels.
All inputs are finite; a program needn't handle non-finite values. No bound on the sum of `ocean_mask` on one device may be relied on, other than what follows from the above.
Results may differ from the reference program's by a relative error of at most 0.00002.
Values sent between devices are 32-bit elements; how exact they have to be, the bound alone decides.
No kernel may reach another device: no remote copies, remote signals or barrier semaphores. Data moves between devices by JAX's collectives and lax.ppermute only.
A program may use at most 64 MiB of HBM per device.

```python
import math
import jax
import jax.numpy as jnp

STEPS = 16
SWEEPS = 2
DCLASS = 32
NY = 1088
NX = 3072
N_TM = 8


def set_ends(array, rng, smallest, top_value):
    shape = array.shape
    place = [jax.random.randint(jax.random.fold_in(rng, axis), (), 0, shape[axis]) for axis in range(len(shape))]
    array = array.at[tuple(place)].set(smallest)
    longest = shape.index(max(shape))
    place[longest] = (place[longest] + 1) % shape[longest]
    return array.at[tuple(place)].set(top_value)


def levels(key, dims, pieces, least, largest):
    level, own = 1.0, jax.random.fold_in(key, 6)
    for position, parts in pieces:
        heights = jnp.exp(jax.random.uniform(jax.random.fold_in(own, position), (parts,), jnp.float32, least / len(pieces), largest / len(pieces)))
        level = level * jnp.repeat(heights, dims[position] // parts).reshape([-1 if axis == position else 1 for axis in range(len(dims))])
    return level


def centred(own_key, extent, width, reach, split=(), held_as=jnp.bfloat16):
    result = width * jax.random.normal(own_key, extent, jnp.float32)
    if split:
        result = result * levels(own_key, extent, split, -0.22, 0.18)
    return jnp.clip(result, -reach, reach).astype(held_as)


def setup_inputs(seed: int = 0) -> dict:
    splits = jax.random.split(jax.random.key(seed), 8)
    return {
        "depth_class": set_ends(jax.random.randint(splits[0], (NY, NX), 0, DCLASS), jax.random.fold_in(splits[0], 1), 0, DCLASS - 1).astype(jnp.int32),
        "ocean_mask": set_ends((jax.random.randint(splits[1], (NY, NX), 0, 10) < 7).astype(jnp.int32), jax.random.fold_in(splits[1], 1), 0, 1),
        "depth_levels": jnp.clip(jnp.exp(jax.random.uniform(splits[2], (DCLASS,), jnp.float32, math.log(0.1), math.log(1.0))), 0.1, 1.0),
        "drag": jnp.clip(jnp.exp(math.log(0.02) - 3.6888794 * jax.random.uniform(splits[3], (NY, NX), jnp.float32) ** levels(splits[3], (NY, NX), ((0, 8), (1, 8)), -0.2, 0.2)), 0.0005, 0.02),
        "tide_force": centred(splits[4], (2, NY, NX), 1.0, 6.0, ((1, 8), (2, 8)), jnp.float32),
        "forward_flow": centred(splits[5], (4, NY, NX), 1.0, 6.0, ((1, 8), (2, 8)), jnp.float32),
        "guess": centred(splits[6], (N_TM, 3, NY, NX), 0.5, 4.0, ((0, 8), (2, 8), (3, 8)), jnp.float32),
    }


def west(x):
    return jnp.roll(x, 1, axis=1)


def east(x):
    return jnp.roll(x, -1, axis=1)


def south(x):
    return jnp.roll(x, 1, axis=0)


def north(x):
    return jnp.roll(x, -1, axis=0)


def reference(depth_class, ocean_mask, depth_levels, drag, tide_force, forward_flow, guess):
    ny = ocean_mask.shape[0]
    classes = jnp.arange(DCLASS, dtype=jnp.int32)
    depth = jnp.sum(jnp.where(depth_class[None] == classes[:, None, None], depth_levels[:, None, None], jnp.float32(0.0)), axis=0)
    rows = jnp.arange(ny, dtype=jnp.int32)
    polar = (rows == 0) | (rows == ny - 1)
    mask = jnp.where(polar[:, None], 0, ocean_mask).astype(jnp.float32)
    hu = 0.5 * (depth + west(depth))
    mu = mask * west(mask)
    du = 1.0 - (drag + west(drag)) / (depth + west(depth))
    hv = 0.5 * (depth + south(depth))
    mv = mask * south(mask)
    dv = 1.0 - (drag + south(drag)) / (depth + south(depth))
    weight = mask / depth
    gain = jnp.stack([mask, mu * du ** STEPS, mv * dv ** STEPS])
    cycle = jnp.float32(N_TM * STEPS)

    def fine(state, slice_index, want):
        elev, zonal, merid = state[0], state[1], state[2]
        term = jnp.zeros_like(elev)
        for sub in range(STEPS):
            count = slice_index * STEPS + sub + 1
            angle = jnp.float32(2.0 * math.pi) * jnp.float32(count) / cycle
            cosine, sine = jnp.cos(angle), jnp.sin(angle)
            zonal = mu * (du * zonal - 0.7 * (elev - west(elev)))
            merid = mv * (dv * merid - 0.7 * (elev - south(elev)))
            flux_u = hu * zonal
            flux_v = hv * merid
            spread = (east(flux_u) - flux_u) + (north(flux_v) - flux_v)
            source = tide_force[0] * cosine + tide_force[1] * sine
            elev = mask * (elev - 0.6 * spread + source)
            if want:
                flow_u = forward_flow[0] * cosine + forward_flow[1] * sine
                flow_v = forward_flow[2] * cosine + forward_flow[3] * sine
                u_mid = 0.5 * (zonal + east(zonal))
                v_mid = 0.5 * (merid + north(merid))
                term = term + weight * (flow_u * u_mid + flow_v * v_mid)
        return jnp.stack([elev, zonal, merid]), term

    bounds = [guess[k] for k in range(N_TM)]
    total = jnp.zeros_like(depth)
    for sweep in range(SWEEPS):
        want = sweep == SWEEPS - 1
        ends = []
        for k in range(N_TM):
            end, term = fine(bounds[k], k, want)
            ends.append(end)
            if want:
                total = total + term
        jumps = [ends[(k - 1) % N_TM] - bounds[k] for k in range(N_TM)]
        change = jumps[0]
        fresh = [bounds[0] + change]
        for k in range(1, N_TM):
            change = jumps[k] + gain * change
            fresh.append(bounds[k] + change)
        bounds = fresh
    final_state = jnp.stack(bounds)
    drag_gradient = total / jnp.float32(N_TM * STEPS)
    return final_state, drag_gradient
```

```python
import functools
import math

import jax
import jax.numpy as jnp
import numpy as np
from jax import lax
from jax.experimental import pallas as pl
from jax.experimental.pallas import tpu as pltpu
from jax.sharding import PartitionSpec as P

STEPS = 16
NTM = 8
ROWS = 136
COLS = 384
HALO = 32
EROWS = ROWS + 2 * HALO
ECOLS = 512
NB = EROWS // 8
CROWS = 104
CB = CROWS // 8
OROWS = 72
CHUNK = 96
VMEM = pl.BlockSpec(memory_space=pltpu.VMEM)
SMEM = pl.BlockSpec(memory_space=pltpu.SMEM)
F32 = jnp.float32


def lanes(shape):
    return lax.broadcasted_iota(jnp.int32, shape, 1)


def rows_of(shape):
    return lax.broadcasted_iota(jnp.int32, shape, 0)


def turned(value, shift, axis):
    size = value.shape[axis]
    shift = shift % size
    return value if shift == 0 else pltpu.roll(value, shift, axis)


def call(kernel, out_shapes, scratch, specs):
    outs = tuple(jax.ShapeDtypeStruct(s, F32) for s in out_shapes)
    return pl.pallas_call(
        kernel,
        out_shape=outs,
        in_specs=specs,
        out_specs=tuple(VMEM for _ in outs),
        scratch_shapes=scratch,
        compiler_params=pltpu.CompilerParams(vmem_limit_bytes=60 * 1024 * 1024),
    )


def first_kernel(where_ref, levels, cls_ref, ocean_ref, drag_ref, force_ref, guess_ref, depth_ref, mask_ref, low_ref, high_ref):
    level = [levels[i] for i in range(32)]
    first, last = (where_ref[0], where_ref[1])

    def band(b, carry):
        at = pl.ds(pl.multiple_of(b * 8, 8), 8)
        cls = cls_ref[at, :]
        row = rows_of(cls.shape) + b * 8
        vals = level
        for bit in range(5):
            odd = (cls & (1 << bit)) != 0
            vals = [jnp.where(odd, vals[2 * i + 1], vals[2 * i]) for i in range(len(vals) // 2)]
        depth_ref[at, :] = vals[0]
        polar = (row == first) | (row == last)
        mask_ref[at, :] = jnp.where(polar, 0.0, ocean_ref[at, :].astype(F32))
        return carry

    lax.fori_loop(0, ROWS // 8, band, 0)
    for out, start in ((low_ref, 0), (high_ref, ROWS - HALO)):
        at = slice(start, start + HALO)
        out[0] = depth_ref[at, :]
        out[1] = mask_ref[at, :]
        out[2] = drag_ref[at, :]
        out[3] = force_ref[0, at, :]
        out[4] = force_ref[1, at, :]
        for f in range(3):
            out[5 + f] = guess_ref[f, at, :]


def own_fields(depth_ref, mask_ref, drag_ref, force_ref, guess_ref):
    views = [depth_ref, mask_ref, drag_ref, force_ref.at[0], force_ref.at[1]]
    return views + [guess_ref.at[f] for f in range(3)]


def strip_kernel(depth_ref, mask_ref, drag_ref, force_ref, guess_ref, south_ref, north_ref, west_ref, east_ref):
    own = own_fields(depth_ref, mask_ref, drag_ref, force_ref, guess_ref)
    parts = ((0, HALO, 0), (HALO, ROWS, 1), (HALO + ROWS, HALO, 2))
    for start, size, kind in parts:
        for out, tile, base in ((west_ref, 0, 0), (east_ref, COLS - 128, 96)):
            for half in range(2):
                lane = lanes((size, 128))
                packed = None
                for j in range(4):
                    f = half * 4 + j
                    src = (south_ref.at[f], own[f], north_ref.at[f])[kind]
                    piece = turned(src[:, tile : tile + 128], j * 32 - base, 1)
                    packed = piece if j == 0 else jnp.where(lane >= j * 32, piece, packed)
                out[start : start + size, half * 128 : half * 128 + 128] = packed


def south(block, before, row):
    return jnp.where(row == 0, turned(before, 1, 0), turned(block, 1, 0))


def power16(x):
    for _ in range(4):
        x = x * x
    return x


def window(ref_rows, start, tiles):
    t, r = divmod(start % (128 * tiles), 128)
    left = turned(ref_rows(t), -r, 1)
    right = turned(ref_rows((t + 1) % tiles), -r, 1)
    return jnp.where(lanes(left.shape) < 128 - r, left, right)


def sweep_kernel(
    info_ref, wave_ref, depth_ref, mask_ref, drag_ref, force_ref, guess_ref, flow_ref, south_ref, north_ref,
    from_west, from_east, out_ref, fixed_ref, flows_ref, raw, fixed, gone,
):
    own = own_fields(depth_ref, mask_ref, drag_ref, force_ref, guess_ref)
    k, keep, cy, cx = (info_ref[0], info_ref[1], info_ref[2], info_ref[3])
    for f in range(8):
        raw[f, 0:HALO, 0:COLS] = south_ref[f]
        raw[f, HALO : HALO + ROWS, 0:COLS] = own[f][...]
        raw[f, HALO + ROWS :, 0:COLS] = north_ref[f]
        j, at = (f % 4, slice(f // 4 * 128, f // 4 * 128 + 128))
        east = turned(from_east[:, at], -j * 32, 1)
        west = turned(from_west[:, at], 96 - j * 32, 1)
        lane = lanes(east.shape)
        raw[f, :, COLS:] = jnp.where(lane < 32, east, jnp.where(lane >= 96, west, 0.0))

    row = rows_of((8, ECOLS))
    keepf = keep.astype(F32)

    def prepare(b, carry):
        at = pl.ds(pl.multiple_of(b * 8, 8), 8)
        up = pl.ds(pl.multiple_of(lax.rem(b + NB - 1, NB) * 8, 8), 8)

        def pair(f):
            x = raw[f, at, :]
            before = raw[f, up, :]
            if f == 0:
                x = jnp.where(x > 0.0, x, 1.0)
                before = jnp.where(before > 0.0, before, 1.0)
            return x, turned(x, 1, 1), south(x, before, row)

        dep, dep_w, dep_s = pair(0)
        m, m_w, m_s = pair(1)
        dr, dr_w, dr_s = pair(2)
        mu, mv = (m * m_w, m * m_s)
        mdu = mu * (1.0 - (dr + dr_w) / (dep + dep_w))
        mdv = mv * (1.0 - (dr + dr_s) / (dep + dep_s))
        fixed[0, at, :] = mdu
        fixed[1, at, :] = 0.7 * mu
        fixed[2, at, :] = 0.3 * (dep + dep_w)
        fixed[3, at, :] = mdv
        fixed[4, at, :] = 0.7 * mv
        fixed[5, at, :] = 0.3 * (dep + dep_s)
        fixed[6, at, :] = m
        fixed[7, at, :] = m * raw[3, at, :]
        fixed[8, at, :] = m * raw[4, at, :]
        fixed[9, at, :] = 0.5 * m / dep
        elev = m * raw[5, at, :]
        gone[0, at, :] = keepf * elev
        gone[1, at, :] = keepf * (power16(mdu) * raw[6, at, :])
        gone[2, at, :] = keepf * (power16(mdv) * raw[7, at, :])
        return carry

    lax.fori_loop(0, NB, prepare, 0)
    for b in range(NB):
        at = slice(b * 8, b * 8 + 8)
        raw[5, at, :] = fixed[6, at, :] * raw[5, at, :]

    def step(s, carry):
        c, z = (wave_ref[0, k * STEPS + s], wave_ref[1, k * STEPS + s])
        a = raw[5, (NB - 1) * 8 :, :]
        turned_a = turned(a, 1, 0)
        after = jnp.zeros((8, ECOLS), F32)
        for b in range(NB - 1, -1, -1):
            at = slice(b * 8, b * 8 + 8)
            if b > 0:
                a_before = raw[5, b * 8 - 8 : b * 8, :]
                turned_before = turned(a_before, 1, 0)
            else:
                a_before, turned_before = (a, turned_a)
            a_s = jnp.where(row == 0, turned_before, turned_a)
            p = fixed[0, at, :] * raw[6, at, :] - fixed[1, at, :] * (a - turned(a, 1, 1))
            q = fixed[3, at, :] * raw[7, at, :] - fixed[4, at, :] * (a - a_s)
            raw[6, at, :] = p
            raw[7, at, :] = q
            fu, fv = (fixed[2, at, :] * p, fixed[5, at, :] * q)
            turned_fv = turned(fv, -1, 0)
            n_fv = jnp.where(row == 7, after, turned_fv)
            spread = (turned(fu, -1, 1) - fu) + (n_fv - fv)
            source = fixed[7, at, :] * c + fixed[8, at, :] * z
            raw[5, at, :] = (a + source) - fixed[6, at, :] * spread
            a, turned_a, after = (a_before, turned_before, turned_fv)
        return carry

    lax.fori_loop(0, STEPS, step, 0)
    for b in range(2, NB - 2):
        at = slice(b * 8, b * 8 + 8)
        for f in range(3):
            raw[5 + f, at, :] = raw[5 + f, at, :] - gone[f, at, :]

    for y in range(2):
        for f in range(3):
            at = slice(16 + 64 * y, 16 + 64 * y + CROWS)
            for x in range(4):
                tile = window(lambda t: raw[5 + f, at, t * 128 : t * 128 + 128], 96 * x - 16, 4)
                out_ref[y * 4 + x, f * CROWS : (f + 1) * CROWS, :] = tile

    top = pl.ds(pl.multiple_of(16 + 64 * cy, 8), CROWS)
    mid = pl.ds(pl.multiple_of(64 * cy, 8), OROWS)
    for x in range(4):

        @pl.when(cx == x)
        def _(x=x):
            for f in range(10):
                fixed_ref[f] = window(lambda t: fixed[f, top, t * 128 : t * 128 + 128], 96 * x - 16, 4)
            for f in range(4):
                flows_ref[f] = window(lambda t: flow_ref[f, mid, t * 128 : t * 128 + 128], 96 * x - 16, 3)


def last_kernel(wave_ref, got_ref, fixed, flows_ref, out_ref, state, old, sums):
    row = rows_of((8, 128))

    def start(b, carry):
        at = pl.ds(pl.multiple_of(b * 8, 8), 8)
        gain = (fixed[6, at, :], power16(fixed[0, at, :]), power16(fixed[3, at, :]))
        for f in range(3):
            line = pl.ds(pl.multiple_of(f * CROWS + b * 8, 8), 8)
            now = got_ref[NTM - 1, line, :]
            for k in range(NTM):
                if k > 0:
                    now = got_ref[k - 1, line, :] + gain[f] * now
                state[k, f, at, :] = now
                old[k, f, at, :] = gain[f] * now
        return carry

    lax.fori_loop(0, CB, start, 0)
    for i in range(4):
        sums[i] = jnp.zeros((CROWS, 128), F32)

    def step(s, carry):
        cs = [wave_ref[0, k * STEPS + s] for k in range(NTM)]
        zs = [wave_ref[1, k * STEPS + s] for k in range(NTM)]
        after = [jnp.zeros((8, 128), F32)] * NTM
        for b in range(CB - 1, -1, -1):
            at = slice(b * 8, b * 8 + 8)
            mdu, mu7, hu, mdv, mv7, hv, m, f0, f1 = [fixed[i, at, :] for i in range(9)]
            inside = 2 <= b <= 11
            if inside:
                total = [sums[i, at, :] for i in range(4)]
            for k in range(NTM):
                c, z = (cs[k], zs[k])
                a = state[k, 0, at, :]
                before = state[k, 0, b * 8 - 8 : b * 8, :] if b > 0 else a
                a_s = south(a, before, row)
                p = mdu * state[k, 1, at, :] - mu7 * (a - turned(a, 1, 1))
                q = mdv * state[k, 2, at, :] - mv7 * (a - a_s)
                state[k, 1, at, :] = p
                state[k, 2, at, :] = q
                if inside:
                    total[0] = total[0] + c * p
                    total[1] = total[1] + z * p
                    total[2] = total[2] + c * q
                    total[3] = total[3] + z * q
                fu, fv = (hu * p, hv * q)
                turned_fv = turned(fv, -1, 0)
                n_fv = jnp.where(row == 7, after[k], turned_fv)
                spread = (turned(fu, -1, 1) - fu) + (n_fv - fv)
                state[k, 0, at, :] = (a + (f0 * c + f1 * z)) - m * spread
                after[k] = turned_fv
            if inside:
                for i in range(4):
                    sums[i, at, :] = total[i]
        return carry

    lax.fori_loop(0, STEPS, step, 0)

    lane = lanes((8, 128))
    for b in range(OROWS // 8):
        at = slice(16 + b * 8, 24 + b * 8)
        down = slice(24 + b * 8, 32 + b * 8)
        here = slice(b * 8, b * 8 + 8)
        grad = None
        for i in range(4):
            x = sums[i, at, :]
            if i < 2:
                mid = x + turned(x, -1, 1)
            else:
                mid = x + jnp.where(row == 7, turned(sums[i, down, :], -1, 0), turned(x, -1, 0))
            part = flows_ref[i, here, :] * mid
            grad = part if grad is None else grad + part
        grad = turned(fixed[9, at, :] * grad * (1.0 / (NTM * STEPS)), 16, 1)
        gain = (fixed[6, at, :], power16(fixed[0, at, :]), power16(fixed[3, at, :]))
        now = [state[NTM - 1, f, at, :] for f in range(3)]
        for k in range(NTM):
            if k > 0:
                now = [
                    (state[k - 1, f, at, :] - old[k - 1, f, at, :]) + gain[f] * now[f] for f in range(3)
                ]
            a, p, q = (turned(now[0], -16, 1), turned(now[1], 80, 1), turned(now[2], 48, 1))
            out_ref[k, here, 0:128] = jnp.where(lane < 96, a, p)
            out_ref[k, here, 128:256] = jnp.where(lane < 64, p, q)
            out_ref[k, here, 256:384] = jnp.where(lane < 32, q, grad)


def unpack_kernel(got_ref, state_ref, grad_ref):
    lane = lanes((8, COLS))
    for b in range(ROWS // 8):
        y = 0 if b < OROWS // 8 else 1
        at = slice(b * 8 - 64 * y, b * 8 - 64 * y + 8)
        here = slice(b * 8, b * 8 + 8)
        parts = [got_ref[y * 4 + x, at, :] for x in range(4)]
        for f in range(4):
            value = turned(parts[0], -CHUNK * f, 1)
            for x in range(1, 4):
                value = jnp.where(lane >= CHUNK * x, turned(parts[x], CHUNK * (x - f), 1), value)
            if f < 3:
                state_ref[f, here, :] = value
            else:
                grad_ref[here, :] = value


def waves():
    count = np.arange(1, NTM * STEPS + 1, dtype=np.float32)
    angle = np.float32(2.0 * math.pi) * count / np.float32(NTM * STEPS)
    return np.stack([np.cos(angle), np.sin(angle)]).astype(np.float32)


def shards(depth_class, ocean_mask, depth_levels, drag, tide_force, forward_flow, guess):
    guess = guess[0]
    lat, lat_size = (lax.axis_index("lat"), lax.axis_size("lat"))
    k = lax.axis_index("tm")
    never = jnp.int32(-1)
    ends = jnp.stack([jnp.where(lat == 0, 0, never), jnp.where(lat == lat_size - 1, ROWS - 1, never)])
    info = jnp.stack([k, jnp.where(k == NTM - 1, 0, 1), k // 4, k % 4]).astype(jnp.int32)
    wave = jnp.asarray(waves())
    block = (ROWS, COLS)
    strip = (8, HALO, COLS)
    depth, mask, low, high = call(
        first_kernel, (block, block, strip, strip), [], [SMEM, SMEM] + [VMEM] * 5
    )(ends, depth_levels, depth_class, ocean_mask, drag, tide_force, guess)
    up = [(i, i + 1) for i in range(lat_size - 1)]
    down = [(i + 1, i) for i in range(lat_size - 1)]
    from_south = lax.ppermute(high, "lat", up)
    from_north = lax.ppermute(low, "lat", down)
    fields = (depth, mask, drag, tide_force, guess)
    side = (EROWS, 256)
    west, east = call(strip_kernel, (side, side), [], [VMEM] * 7)(*fields, from_south, from_north)
    lon_size = lax.axis_size("lon")
    from_west = lax.ppermute(east, "lon", [(i, (i + 1) % lon_size) for i in range(lon_size)])
    from_east = lax.ppermute(west, "lon", [((i + 1) % lon_size, i) for i in range(lon_size)])
    big = (EROWS, ECOLS)
    sent, fixed, flows = call(
        sweep_kernel,
        ((NTM, 3 * CROWS, 128), (10, CROWS, 128), (4, OROWS, 128)),
        [pltpu.VMEM((8, *big), F32), pltpu.VMEM((10, *big), F32), pltpu.VMEM((3, *big), F32)],
        [SMEM, SMEM] + [VMEM] * 10,
    )(info, wave, *fields, forward_flow, from_south, from_north, from_west, from_east)
    got = lax.all_to_all(sent, "tm", 0, 0, tiled=True)
    (back,) = call(
        last_kernel,
        ((NTM, OROWS, COLS),),
        [
            pltpu.VMEM((NTM, 3, CROWS, 128), F32),
            pltpu.VMEM((NTM, 3, CROWS, 128), F32),
            pltpu.VMEM((4, CROWS, 128), F32),
        ],
        [SMEM] + [VMEM] * 3,
    )(wave, got, fixed, flows)
    home = lax.all_to_all(back, "tm", 0, 0, tiled=True)
    state, grad = call(unpack_kernel, ((3, *block), block), [], [VMEM])(home)
    return (state[None], grad)


def solution(mesh):
    return jax.shard_map(
        shards,
        mesh=mesh,
        in_specs=(
            P("lat", "lon"),
            P("lat", "lon"),
            P(),
            P("lat", "lon"),
            P(None, "lat", "lon"),
            P(None, "lat", "lon"),
            P("tm", None, "lat", "lon"),
        ),
        out_specs=(P("tm", None, "lat", "lon"), P("lat", "lon")),
        check_vma=False,
    )
```

```python
import functools
import math

import jax
import jax.numpy as jnp
import numpy as np
from jax import lax
from jax.experimental import pallas as pl
from jax.experimental.pallas import tpu as pltpu
from jax.sharding import PartitionSpec as P

STEPS = 16
NTM = 8
ROWS = 136
COLS = 384
HALO = 32
EROWS = ROWS + 2 * HALO
ECOLS = 512
NB = EROWS // 8
CROWS = 104
CB = CROWS // 8
OROWS = 72
CHUNK = 96
VMEM = pl.BlockSpec(memory_space=pltpu.VMEM)
SMEM = pl.BlockSpec(memory_space=pltpu.SMEM)
F32 = jnp.float32


def lanes(shape):
    return lax.broadcasted_iota(jnp.int32, shape, 1)


def rows_of(shape):
    return lax.broadcasted_iota(jnp.int32, shape, 0)


def turned(value, shift, axis):
    size = value.shape[axis]
    shift = shift % size
    return value if shift == 0 else pltpu.roll(value, shift, axis)


def call(kernel, out_shapes, scratch, specs, mib):
    outs = tuple(jax.ShapeDtypeStruct(s, F32) for s in out_shapes)
    return pl.pallas_call(
        kernel,
        out_shape=outs,
        in_specs=specs,
        out_specs=tuple(VMEM for _ in outs),
        scratch_shapes=scratch,
        compiler_params=pltpu.CompilerParams(vmem_limit_bytes=mib * 1024 * 1024),
    )


def first_kernel(where_ref, levels, cls_ref, ocean_ref, drag_ref, force_ref, guess_ref, depth_ref, mask_ref, low_ref, high_ref):
    level = [levels[i] for i in range(32)]
    first, last = (where_ref[0], where_ref[1])

    def band(b, carry):
        at = pl.ds(pl.multiple_of(b * 8, 8), 8)
        cls = cls_ref[at, :]
        row = rows_of(cls.shape) + b * 8
        vals = level
        for bit in range(5):
            odd = (cls & (1 << bit)) != 0
            vals = [jnp.where(odd, vals[2 * i + 1], vals[2 * i]) for i in range(len(vals) // 2)]
        depth_ref[at, :] = vals[0]
        polar = (row == first) | (row == last)
        mask_ref[at, :] = jnp.where(polar, 0.0, ocean_ref[at, :].astype(F32))
        return carry

    lax.fori_loop(0, ROWS // 8, band, 0)
    for out, start in ((low_ref, 0), (high_ref, ROWS - HALO)):
        at = slice(start, start + HALO)
        out[0] = depth_ref[at, :]
        out[1] = mask_ref[at, :]
        out[2] = drag_ref[at, :]
        out[3] = force_ref[0, at, :]
        out[4] = force_ref[1, at, :]
        for f in range(3):
            out[5 + f] = guess_ref[f, at, :]


def own_fields(depth_ref, mask_ref, drag_ref, force_ref, guess_ref):
    views = [depth_ref, mask_ref, drag_ref, force_ref.at[0], force_ref.at[1]]
    return views + [guess_ref.at[f] for f in range(3)]


def strip_kernel(depth_ref, mask_ref, drag_ref, force_ref, guess_ref, south_ref, north_ref, west_ref, east_ref):
    own = own_fields(depth_ref, mask_ref, drag_ref, force_ref, guess_ref)
    parts = ((0, HALO, 0), (HALO, ROWS, 1), (HALO + ROWS, HALO, 2))
    for start, size, kind in parts:
        for out, tile, base in ((west_ref, 0, 0), (east_ref, COLS - 128, 96)):
            for half in range(2):
                lane = lanes((size, 128))
                packed = None
                for j in range(4):
                    f = half * 4 + j
                    src = (south_ref.at[f], own[f], north_ref.at[f])[kind]
                    piece = turned(src[:, tile : tile + 128], j * 32 - base, 1)
                    packed = piece if j == 0 else jnp.where(lane >= j * 32, piece, packed)
                out[start : start + size, half * 128 : half * 128 + 128] = packed


def south(block, before, row):
    return jnp.where(row == 0, turned(before, 1, 0), turned(block, 1, 0))


def power16(x):
    for _ in range(4):
        x = x * x
    return x


def window(ref_rows, start, tiles):
    t, r = divmod(start % (128 * tiles), 128)
    left = turned(ref_rows(t), -r, 1)
    right = turned(ref_rows((t + 1) % tiles), -r, 1)
    return jnp.where(lanes(left.shape) < 128 - r, left, right)


def sweep_kernel(
    info_ref, wave_ref, depth_ref, mask_ref, drag_ref, force_ref, guess_ref, flow_ref, south_ref, north_ref,
    from_west, from_east, out_ref, fixed_ref, flows_ref, raw, fixed, gone, flux,
):
    own = own_fields(depth_ref, mask_ref, drag_ref, force_ref, guess_ref)
    k, keep, cy, cx = (info_ref[0], info_ref[1], info_ref[2], info_ref[3])
    for f in range(8):
        raw[f, 0:HALO, 0:COLS] = south_ref[f]
        raw[f, HALO : HALO + ROWS, 0:COLS] = own[f][...]
        raw[f, HALO + ROWS :, 0:COLS] = north_ref[f]
        j, at = (f % 4, slice(f // 4 * 128, f // 4 * 128 + 128))
        east = turned(from_east[:, at], -j * 32, 1)
        west = turned(from_west[:, at], 96 - j * 32, 1)
        lane = lanes(east.shape)
        raw[f, :, COLS:] = jnp.where(lane < 32, east, jnp.where(lane >= 96, west, 0.0))

    row = rows_of((8, ECOLS))
    keepf = keep.astype(F32)

    def prepare(b, carry):
        at = pl.ds(pl.multiple_of(b * 8, 8), 8)
        up = pl.ds(pl.multiple_of(lax.rem(b + NB - 1, NB) * 8, 8), 8)

        def pair(f):
            x = raw[f, at, :]
            before = raw[f, up, :]
            if f == 0:
                x = jnp.where(x > 0.0, x, 1.0)
                before = jnp.where(before > 0.0, before, 1.0)
            return x, turned(x, 1, 1), south(x, before, row)

        dep, dep_w, dep_s = pair(0)
        m, m_w, m_s = pair(1)
        dr, dr_w, dr_s = pair(2)
        mu, mv = (m * m_w, m * m_s)
        mdu = mu * (1.0 - (dr + dr_w) / (dep + dep_w))
        mdv = mv * (1.0 - (dr + dr_s) / (dep + dep_s))
        hu, hv = (0.3 * (dep + dep_w), 0.3 * (dep + dep_s))
        fixed[0, at, :] = mdu
        fixed[1, at, :] = (0.7 * mu) * hu
        fixed[2, at, :] = mdv
        fixed[3, at, :] = (0.7 * mv) * hv
        fixed[4, at, :] = m * raw[3, at, :]
        fixed[5, at, :] = m * raw[4, at, :]
        fixed[6, at, :] = hu
        fixed[7, at, :] = hv
        fixed[8, at, :] = m
        fixed[9, at, :] = 0.5 * m / dep
        elev, zonal, merid = (m * raw[5, at, :], raw[6, at, :], raw[7, at, :])
        flux[0, at, :] = elev
        flux[1, at, :] = hu * zonal
        flux[2, at, :] = hv * merid
        gone[0, at, :] = keepf * elev
        gone[1, at, :] = keepf * (power16(mdu) * zonal)
        gone[2, at, :] = keepf * (power16(mdv) * merid)
        return carry

    lax.fori_loop(0, NB, prepare, 0)
    def step(s, carry):
        c, z = (wave_ref[0, k * STEPS + s], wave_ref[1, k * STEPS + s])
        a = flux[0, EROWS - 8 :, :]
        turned_a = turned(a, 1, 0)
        after = jnp.zeros((8, ECOLS), F32)
        for b in range(NB - 1, -1, -1):
            at = slice(b * 8, b * 8 + 8)
            a_before = flux[0, b * 8 - 8 : b * 8, :] if b > 0 else a
            turned_before = turned(a_before, 1, 0) if b > 0 else turned_a
            a_s = jnp.where(row == 0, turned_before, turned_a)
            u = fixed[0, at, :] * flux[1, at, :] - fixed[1, at, :] * (a - turned(a, 1, 1))
            v = fixed[2, at, :] * flux[2, at, :] - fixed[3, at, :] * (a - a_s)
            flux[1, at, :] = u
            flux[2, at, :] = v
            turned_v = turned(v, -1, 0)
            v_n = jnp.where(row == 7, after, turned_v)
            source = fixed[4, at, :] * c + fixed[5, at, :] * z
            flux[0, at, :] = (a + source) - ((turned(u, -1, 1) - u) + (v_n - v))
            a, turned_a, after = (a_before, turned_before, turned_v)
        return carry

    lax.fori_loop(0, STEPS, step, 0)
    for b in range(2, NB - 2):
        at = slice(b * 8, b * 8 + 8)
        flux[0, at, :] = flux[0, at, :] - gone[0, at, :]
        flux[1, at, :] = flux[1, at, :] / fixed[6, at, :] - gone[1, at, :]
        flux[2, at, :] = flux[2, at, :] / fixed[7, at, :] - gone[2, at, :]

    for y in range(2):
        for f in range(3):
            at = slice(16 + 64 * y, 16 + 64 * y + CROWS)
            for x in range(4):
                tile = window(lambda t: flux[f, at, t * 128 : t * 128 + 128], 96 * x - 16, 4)
                out_ref[y * 4 + x, f * CROWS : (f + 1) * CROWS, :] = tile

    top = pl.ds(pl.multiple_of(16 + 64 * cy, 8), CROWS)
    mid = pl.ds(pl.multiple_of(64 * cy, 8), OROWS)
    for x in range(4):

        @pl.when(cx == x)
        def _(x=x):
            for f in range(10):
                fixed_ref[f] = window(lambda t: fixed[f, top, t * 128 : t * 128 + 128], 96 * x - 16, 4)
            for f in range(4):
                flows_ref[f] = window(lambda t: flow_ref[f, mid, t * 128 : t * 128 + 128], 96 * x - 16, 3)


def last_kernel(wave_ref, got_ref, fixed, flows_ref, out_ref, state, old, sums):
    row = rows_of((8, 128))

    def gains(at):
        return (fixed[8, at, :], power16(fixed[0, at, :]), power16(fixed[2, at, :]))

    def start(b, carry):
        at = pl.ds(pl.multiple_of(b * 8, 8), 8)
        gain = gains(at)
        scale = (None, fixed[6, at, :], fixed[7, at, :])
        for f in range(3):
            line = pl.ds(pl.multiple_of(f * CROWS + b * 8, 8), 8)
            now = got_ref[NTM - 1, line, :]
            for k in range(NTM):
                if k > 0:
                    now = got_ref[k - 1, line, :] + gain[f] * now
                state[k, f, at, :] = now if f == 0 else scale[f] * now
                old[k, f, at, :] = gain[f] * now
        return carry

    lax.fori_loop(0, CB, start, 0)
    for i in range(4):
        sums[i] = jnp.zeros((CROWS, 128), F32)
    half = math.sqrt(0.5)

    def step(s, carry):
        c, z = (wave_ref[0, s], wave_ref[1, s])
        for b in range(CB - 1, -1, -1):
            at = slice(b * 8, b * 8 + 8)
            mdu, ku, mdv, kv, f0, f1 = [fixed[i, at, :] for i in range(6)]
            even, odd = (f0 * c + f1 * z, f1 * c - f0 * z)
            source = (even, half * (odd + even), odd, half * (odd - even))
            split = ([None] * NTM, [None] * NTM)
            for k in (0, 4, 1, 5, 2, 6, 3, 7):
                a = state[k, 0, at, :]
                a_s = state[k, 0, b * 8 - 1 : b * 8 + 7, :] if b > 0 else turned(a, 1, 0)
                u = mdu * state[k, 1, at, :] - ku * (a - turned(a, 1, 1))
                v = mdv * state[k, 2, at, :] - kv * (a - a_s)
                state[k, 1, at, :] = u
                state[k, 2, at, :] = v
                v_n = state[k, 2, b * 8 + 1 : b * 8 + 9, :] if b < CB - 1 else turned(v, -1, 0)
                forced = a + source[k] if k < 4 else a - source[k - 4]
                state[k, 0, at, :] = forced - ((turned(u, -1, 1) - u) + (v_n - v))
                for part, value in zip(split, (u, v)):
                    if k < 4:
                        part[k] = value
                    else:
                        part[k - 4] = part[k - 4] - value
            if 2 <= b <= 11:
                for i in range(2):
                    w = split[i]
                    x = w[0] + half * (w[1] - w[3])
                    y = w[2] + half * (w[1] + w[3])
                    sums[2 * i, at, :] = sums[2 * i, at, :] + (c * x - z * y)
                    sums[2 * i + 1, at, :] = sums[2 * i + 1, at, :] + (z * x + c * y)
        return carry

    lax.fori_loop(0, STEPS, step, 0)
    for b in range(2, 12):
        at = slice(b * 8, b * 8 + 8)
        for i in range(4):
            sums[i, at, :] = sums[i, at, :] / fixed[6 + i // 2, at, :]

    lane = lanes((8, 128))
    for b in range(OROWS // 8):
        at = slice(16 + b * 8, 24 + b * 8)
        here = slice(b * 8, b * 8 + 8)
        grad = None
        for i in range(4):
            x = sums[i, at, :]
            if i < 2:
                mid = x + turned(x, -1, 1)
            else:
                mid = x + sums[i, 17 + b * 8 : 25 + b * 8, :]
            part = flows_ref[i, here, :] * mid
            grad = part if grad is None else grad + part
        grad = turned(fixed[9, at, :] * grad * (1.0 / (NTM * STEPS)), 16, 1)
        gain = gains(at)
        scale = (None, 1.0 / fixed[6, at, :], 1.0 / fixed[7, at, :])

        def end(k, f):
            value = state[k, f, at, :]
            return value if f == 0 else value * scale[f]

        now = [end(NTM - 1, f) for f in range(3)]
        for k in range(NTM):
            if k > 0:
                now = [(end(k - 1, f) - old[k - 1, f, at, :]) + gain[f] * now[f] for f in range(3)]
            a, p, q = (turned(now[0], -16, 1), turned(now[1], 80, 1), turned(now[2], 48, 1))
            out_ref[k, here, 0:128] = jnp.where(lane < 96, a, p)
            out_ref[k, here, 128:256] = jnp.where(lane < 64, p, q)
            out_ref[k, here, 256:384] = jnp.where(lane < 32, q, grad)


def unpack_kernel(got_ref, state_ref, grad_ref):
    lane = lanes((8, COLS))
    for b in range(ROWS // 8):
        y = 0 if b < OROWS // 8 else 1
        at = slice(b * 8 - 64 * y, b * 8 - 64 * y + 8)
        here = slice(b * 8, b * 8 + 8)
        parts = [got_ref[y * 4 + x, at, :] for x in range(4)]
        for f in range(4):
            value = turned(parts[0], -CHUNK * f, 1)
            for x in range(1, 4):
                value = jnp.where(lane >= CHUNK * x, turned(parts[x], CHUNK * (x - f), 1), value)
            if f < 3:
                state_ref[f, here, :] = value
            else:
                grad_ref[here, :] = value


def waves():
    count = np.arange(1, NTM * STEPS + 1, dtype=np.float32)
    angle = np.float32(2.0 * math.pi) * count / np.float32(NTM * STEPS)
    return np.stack([np.cos(angle), np.sin(angle)]).astype(np.float32)


def shards(depth_class, ocean_mask, depth_levels, drag, tide_force, forward_flow, guess):
    guess = guess[0]
    lat, lat_size = (lax.axis_index("lat"), lax.axis_size("lat"))
    k = lax.axis_index("tm")
    never = jnp.int32(-1)
    ends = jnp.stack([jnp.where(lat == 0, 0, never), jnp.where(lat == lat_size - 1, ROWS - 1, never)])
    info = jnp.stack([k, jnp.where(k == NTM - 1, 0, 1), k // 4, k % 4]).astype(jnp.int32)
    wave = jnp.asarray(waves())
    block = (ROWS, COLS)
    strip = (8, HALO, COLS)
    depth, mask, low, high = call(
        first_kernel, (block, block, strip, strip), [], [SMEM, SMEM] + [VMEM] * 5, 6
    )(ends, depth_levels, depth_class, ocean_mask, drag, tide_force, guess)
    up = [(i, i + 1) for i in range(lat_size - 1)]
    down = [(i + 1, i) for i in range(lat_size - 1)]
    from_south = lax.ppermute(high, "lat", up)
    from_north = lax.ppermute(low, "lat", down)
    fields = (depth, mask, drag, tide_force, guess)
    side = (EROWS, 256)
    west, east = call(strip_kernel, (side, side), [], [VMEM] * 7, 6)(*fields, from_south, from_north)
    lon_size = lax.axis_size("lon")
    from_west = lax.ppermute(east, "lon", [(i, (i + 1) % lon_size) for i in range(lon_size)])
    from_east = lax.ppermute(west, "lon", [((i + 1) % lon_size, i) for i in range(lon_size)])
    big = (EROWS, ECOLS)
    sent, fixed, flows = call(
        sweep_kernel,
        ((NTM, 3 * CROWS, 128), (10, CROWS, 128), (4, OROWS, 128)),
        [pltpu.VMEM((8, *big), F32), pltpu.VMEM((10, *big), F32), pltpu.VMEM((3, *big), F32), pltpu.VMEM((3, *big), F32)],
        [SMEM, SMEM] + [VMEM] * 10,
        20,
    )(info, wave, *fields, forward_flow, from_south, from_north, from_west, from_east)
    got = lax.all_to_all(sent, "tm", 0, 0, tiled=True)
    (back,) = call(
        last_kernel,
        ((NTM, OROWS, COLS),),
        [
            pltpu.VMEM((NTM, 3, CROWS, 128), F32),
            pltpu.VMEM((NTM, 3, CROWS, 128), F32),
            pltpu.VMEM((4, CROWS, 128), F32),
        ],
        [SMEM] + [VMEM] * 3,
        10,
    )(wave, got, fixed, flows)
    home = lax.all_to_all(back, "tm", 0, 0, tiled=True)
    state, grad = call(unpack_kernel, ((3, *block), block), [], [VMEM], 6)(home)
    return (state[None], grad)


def solution(mesh):
    return jax.shard_map(
        shards,
        mesh=mesh,
        in_specs=(
            P("lat", "lon"),
            P("lat", "lon"),
            P(),
            P("lat", "lon"),
            P(None, "lat", "lon"),
            P(None, "lat", "lon"),
            P("tm", None, "lat", "lon"),
        ),
        out_specs=(P("tm", None, "lat", "lon"), P("lat", "lon")),
        check_vma=False,
    )
```

```python
import functools
import math

import jax
import jax.numpy as jnp
import numpy as np
from jax import lax
from jax.experimental import pallas as pl
from jax.experimental.pallas import tpu as pltpu
from jax.sharding import PartitionSpec as P

STEPS = 16
NTM = 8
ROWS = 136
COLS = 384
HALO = 32
EROWS = ROWS + 2 * HALO
NB = EROWS // 8
CROWS = 104
CB = CROWS // 8
OROWS = 72
CHUNK = 96
VMEM = pl.BlockSpec(memory_space=pltpu.VMEM)
SMEM = pl.BlockSpec(memory_space=pltpu.SMEM)
F32 = jnp.float32
FLOPS = 60_000_000


def lanes(shape):
    return lax.broadcasted_iota(jnp.int32, shape, 1)


def rows_of(shape):
    return lax.broadcasted_iota(jnp.int32, shape, 0)


def turned(value, shift, axis):
    size = value.shape[axis]
    shift = shift % size
    return value if shift == 0 else pltpu.roll(value, shift, axis)


def call(kernel, out_shapes, scratch, specs, mib, flops=0):
    outs = tuple(jax.ShapeDtypeStruct(s, F32) for s in out_shapes)
    cost = pl.CostEstimate(flops=flops, bytes_accessed=flops // 4, transcendentals=0) if flops else None
    return pl.pallas_call(
        kernel,
        out_shape=outs,
        in_specs=specs,
        out_specs=tuple(VMEM for _ in outs),
        scratch_shapes=scratch,
        cost_estimate=cost,
        compiler_params=pltpu.CompilerParams(vmem_limit_bytes=mib * 1024 * 1024),
    )


def first_kernel(
    lat_size, lat_ref, levels_hbm, cls_hbm, ocean_hbm, drag_hbm, force_hbm, guess_hbm,
    ground_ref, low_ref, high_ref, west_ref, east_ref,
    levels, cls_ref, ocean_ref, drag_ref, force_ref, guess_ref, sems,
):
    pairs = (
        (levels_hbm, levels), (cls_hbm, cls_ref), (ocean_hbm, ocean_ref),
        (drag_hbm, drag_ref), (force_hbm, force_ref), (guess_hbm, guess_ref),
    )
    copies = [pltpu.make_async_copy(src, dst, sems.at[i]) for i, (src, dst) in enumerate(pairs)]
    for copy in copies:
        copy.start()
    for copy in copies[:3]:
        copy.wait()
    level = [levels[i] for i in range(32)]
    lat = lat_ref[0]
    first = jnp.where(lat == 0, 0, -1)
    last = jnp.where(lat == lat_size - 1, ROWS - 1, -1)
    for b in range(ROWS // 8):
        at = slice(b * 8, b * 8 + 8)
        cls = cls_ref[at, :]
        row = rows_of(cls.shape) + b * 8
        vals = level
        for bit in range(5):
            odd = (cls & (1 << bit)) != 0
            vals = [jnp.where(odd, vals[2 * i + 1], vals[2 * i]) for i in range(len(vals) // 2)]
        ground_ref[0, at, :] = vals[0]
        polar = (row == first) | (row == last)
        ground_ref[1, at, :] = jnp.where(polar, 0.0, ocean_ref[at, :].astype(F32))
    for copy in copies[3:]:
        copy.wait()
    own = own_fields(ground_ref, drag_ref, force_ref, guess_ref)
    for out, start in ((low_ref, 0), (high_ref, ROWS - HALO)):
        for f in range(8):
            out[f] = own[f][start : start + HALO, :]
    lane = lanes((ROWS, 128))
    for out, tile, base in ((west_ref, 0, 0), (east_ref, COLS - 128, 96)):
        for half in range(2):
            packed = None
            for j in range(4):
                piece = turned(own[half * 4 + j][:, tile : tile + 128], j * 32 - base, 1)
                packed = piece if j == 0 else jnp.where(lane >= j * 32, piece, packed)
            out[:, half * 128 : half * 128 + 128] = packed


def own_fields(ground_ref, drag_ref, force_ref, guess_ref):
    views = [ground_ref.at[0], ground_ref.at[1], drag_ref, force_ref.at[0], force_ref.at[1]]
    return views + [guess_ref.at[f] for f in range(3)]


def south(block, before, row):
    return jnp.where(row == 0, turned(before, 1, 0), turned(block, 1, 0))


def power16(x):
    for _ in range(4):
        x = x * x
    return x


def prepare(raw, fixed, gone, flux, keepf, row):
    def band(b, carry):
        at = pl.ds(pl.multiple_of(b * 8, 8), 8)
        up = pl.ds(pl.multiple_of(lax.rem(b + NB - 1, NB) * 8, 8), 8)

        def pair(f):
            x = raw[f, at, :]
            before = raw[f, up, :]
            if f == 0:
                x = jnp.where(x > 0.0, x, 1.0)
                before = jnp.where(before > 0.0, before, 1.0)
            return x, turned(x, 1, 1), south(x, before, row)

        dep, dep_w, dep_s = pair(0)
        m, m_w, m_s = pair(1)
        dr, dr_w, dr_s = pair(2)
        mu, mv = (m * m_w, m * m_s)
        mdu = mu * (1.0 - (dr + dr_w) / (dep + dep_w))
        mdv = mv * (1.0 - (dr + dr_s) / (dep + dep_s))
        hu, hv = (0.3 * (dep + dep_w), 0.3 * (dep + dep_s))
        fixed[0, at, :] = mdu
        fixed[1, at, :] = (0.7 * mu) * hu
        fixed[2, at, :] = mdv
        fixed[3, at, :] = (0.7 * mv) * hv
        fixed[4, at, :] = m * raw[3, at, :]
        fixed[5, at, :] = m * raw[4, at, :]
        fixed[6, at, :] = hu
        fixed[7, at, :] = hv
        fixed[8, at, :] = m
        fixed[9, at, :] = 0.5 * m / dep
        elev, zonal, merid = (m * raw[5, at, :], raw[6, at, :], raw[7, at, :])
        flux[0, at, :] = elev
        flux[1, at, :] = hu * zonal
        flux[2, at, :] = hv * merid
        gone[0, at, :] = keepf * elev
        gone[1, at, :] = keepf * (power16(mdu) * zonal)
        gone[2, at, :] = keepf * (power16(mdv) * merid)
        return carry

    lax.fori_loop(0, NB, band, 0, unroll=5)


def fine(fixed, flux, gone, wave_ref, k, row):
    def step(s, carry):
        c, z = (wave_ref[0, k * STEPS + s], wave_ref[1, k * STEPS + s])
        a = flux[0, EROWS - 8 :, :]
        turned_a = turned(a, 1, 0)
        after = jnp.zeros(a.shape, F32)
        for b in range(NB - 1, -1, -1):
            at = slice(b * 8, b * 8 + 8)
            a_before = flux[0, b * 8 - 8 : b * 8, :] if b > 0 else a
            turned_before = turned(a_before, 1, 0) if b > 0 else turned_a
            a_s = jnp.where(row == 0, turned_before, turned_a)
            u = fixed[0, at, :] * flux[1, at, :] - fixed[1, at, :] * (a - turned(a, 1, 1))
            v = fixed[2, at, :] * flux[2, at, :] - fixed[3, at, :] * (a - a_s)
            flux[1, at, :] = u
            flux[2, at, :] = v
            turned_v = turned(v, -1, 0)
            v_n = jnp.where(row == 7, after, turned_v)
            source = fixed[4, at, :] * c + fixed[5, at, :] * z
            flux[0, at, :] = (a + source) - ((turned(u, -1, 1) - u) + (v_n - v))
            a, turned_a, after = (a_before, turned_before, turned_v)
        return carry

    lax.fori_loop(0, STEPS, step, 0)
    for b in range(2, NB - 2):
        at = slice(b * 8, b * 8 + 8)
        flux[0, at, :] = flux[0, at, :] - gone[0, at, :]
        flux[1, at, :] = flux[1, at, :] / fixed[6, at, :] - gone[1, at, :]
        flux[2, at, :] = flux[2, at, :] / fixed[7, at, :] - gone[2, at, :]


def interior_kernel(
    k_ref, wave_ref, ground_ref, drag_ref, force_ref, guess_ref, south_ref, north_ref,
    fixed, flux, raw, gone,
):
    own = own_fields(ground_ref, drag_ref, force_ref, guess_ref)
    k = k_ref[0]
    for f in range(8):
        raw[f, 0:HALO, :] = south_ref[f]
        raw[f, HALO : HALO + ROWS, :] = own[f][...]
        raw[f, HALO + ROWS :, :] = north_ref[f]
    row = rows_of((8, COLS))
    prepare(raw, fixed, gone, flux, jnp.where(k == NTM - 1, 0.0, 1.0), row)
    fine(fixed, flux, gone, wave_ref, k, row)


def shifted_tiles(left, right, start):
    return jnp.where(lanes(left.shape) < 128 - start, turned(left, -start, 1), turned(right, -start, 1))


def chunk_tile(inner, edge, x):
    if x == 0:
        first = edge()
        return jnp.where(lanes(first.shape) < 32, turned(first, -16, 1), turned(inner(0), 16, 1))
    if x == 3:
        first = edge()
        return jnp.where(lanes(first.shape) >= 96, turned(first, 16, 1), turned(inner(2), -16, 1))
    return shifted_tiles(inner(x - 1), inner(x), 96 * x - 16 - 128 * (x - 1))


def edge_kernel(
    k_ref, wave_ref, ground_ref, drag_ref, force_ref, guess_ref, flow_ref, south_ref, north_ref,
    from_west, from_east, corner_south, corner_north, inner_fixed, inner,
    out_ref, fixed_ref, flows_ref, raw, fixed, gone, flux,
):
    own = own_fields(ground_ref, drag_ref, force_ref, guess_ref)
    k = k_ref[0]
    cy, cx = (lax.shift_right_logical(k, 2), k & 3)
    for f in range(8):
        j, at = (f % 4, slice(f // 4 * 128, f // 4 * 128 + 128))
        parts = (
            (0, HALO, south_ref.at[f], corner_south[0:HALO, at], corner_south[HALO:, at]),
            (HALO, ROWS, own[f], from_west[:, at], from_east[:, at]),
            (HALO + ROWS, HALO, north_ref.at[f], corner_north[0:HALO, at], corner_north[HALO:, at]),
        )
        for start, size, mine, west, east in parts:
            lane = lanes((size, 128))
            low = jnp.where(lane < 32, turned(west, -j * 32, 1), turned(mine[:, 0:128], 32, 1))
            high = jnp.where(lane >= 96, turned(east, 96 - j * 32, 1), turned(mine[:, COLS - 128 :], -32, 1))
            raw[f, start : start + size, :] = jnp.where(lane < 64, low, high)
    row = rows_of((8, 128))
    prepare(raw, fixed, gone, flux, jnp.where(k == NTM - 1, 0.0, 1.0), row)
    fine(fixed, flux, gone, wave_ref, k, row)

    for y in range(2):
        at = slice(16 + 64 * y, 16 + 64 * y + CROWS)
        for f in range(3):
            for x in range(4):
                tile = chunk_tile(
                    lambda t: inner[f, at, t * 128 : t * 128 + 128], lambda: flux[f, at, :], x
                )
                out_ref[y * 4 + x, f * CROWS : (f + 1) * CROWS, :] = tile

    top = pl.ds(pl.multiple_of(16 + 64 * cy, 8), CROWS)
    mid = pl.ds(pl.multiple_of(64 * cy, 8), OROWS)
    for x in range(4):

        @pl.when(cx == x)
        def _(x=x):
            for f in range(10):
                fixed_ref[f] = chunk_tile(
                    lambda t: inner_fixed[f, top, t * 128 : t * 128 + 128], lambda: fixed[f, top, :], x
                )
            for f in range(4):
                view = lambda t: flow_ref[f, mid, t * 128 : t * 128 + 128]
                if x == 0:
                    flows_ref[f] = turned(view(0), 16, 1)
                elif x == 3:
                    flows_ref[f] = turned(view(2), -16, 1)
                else:
                    flows_ref[f] = chunk_tile(view, None, x)


def last_kernel(wave_ref, got_ref, fixed, flows_ref, out_ref, state, old, sums):
    row = rows_of((8, 128))

    def gains(at):
        return (fixed[8, at, :], power16(fixed[0, at, :]), power16(fixed[2, at, :]))

    def start(b, carry):
        at = pl.ds(pl.multiple_of(b * 8, 8), 8)
        gain = gains(at)
        scale = (None, fixed[6, at, :], fixed[7, at, :])
        for f in range(3):
            line = pl.ds(pl.multiple_of(f * CROWS + b * 8, 8), 8)
            now = got_ref[NTM - 1, line, :]
            for k in range(NTM):
                if k > 0:
                    now = got_ref[k - 1, line, :] + gain[f] * now
                state[k, f, at, :] = now if f == 0 else scale[f] * now
                old[k, f, at, :] = gain[f] * now
        return carry

    lax.fori_loop(0, CB, start, 0)
    for i in range(4):
        sums[i] = jnp.zeros((CROWS, 128), F32)
    half = math.sqrt(0.5)

    def step(s, carry):
        c, z = (wave_ref[0, s], wave_ref[1, s])
        for b in range(CB - 1, -1, -1):
            at = slice(b * 8, b * 8 + 8)
            mdu, ku, mdv, kv, f0, f1 = [fixed[i, at, :] for i in range(6)]
            even, odd = (f0 * c + f1 * z, f1 * c - f0 * z)
            source = (even, half * (odd + even), odd, half * (odd - even))
            split = ([None] * NTM, [None] * NTM)
            for k in (0, 4, 1, 5, 2, 6, 3, 7):
                a = state[k, 0, at, :]
                a_s = state[k, 0, b * 8 - 1 : b * 8 + 7, :] if b > 0 else turned(a, 1, 0)
                u = mdu * state[k, 1, at, :] - ku * (a - turned(a, 1, 1))
                v = mdv * state[k, 2, at, :] - kv * (a - a_s)
                state[k, 1, at, :] = u
                state[k, 2, at, :] = v
                v_n = state[k, 2, b * 8 + 1 : b * 8 + 9, :] if b < CB - 1 else turned(v, -1, 0)
                forced = a + source[k] if k < 4 else a - source[k - 4]
                state[k, 0, at, :] = forced - ((turned(u, -1, 1) - u) + (v_n - v))
                for part, value in zip(split, (u, v)):
                    if k < 4:
                        part[k] = value
                    else:
                        part[k - 4] = part[k - 4] - value
            if 2 <= b <= 11:
                for i in range(2):
                    w = split[i]
                    x = w[0] + half * (w[1] - w[3])
                    y = w[2] + half * (w[1] + w[3])
                    sums[2 * i, at, :] = sums[2 * i, at, :] + (c * x - z * y)
                    sums[2 * i + 1, at, :] = sums[2 * i + 1, at, :] + (z * x + c * y)
        return carry

    lax.fori_loop(0, STEPS, step, 0)
    for b in range(2, 12):
        at = slice(b * 8, b * 8 + 8)
        for i in range(4):
            sums[i, at, :] = sums[i, at, :] / fixed[6 + i // 2, at, :]

    lane = lanes((8, 128))
    for b in range(OROWS // 8):
        at = slice(16 + b * 8, 24 + b * 8)
        here = slice(b * 8, b * 8 + 8)
        grad = None
        for i in range(4):
            x = sums[i, at, :]
            if i < 2:
                mid = x + turned(x, -1, 1)
            else:
                mid = x + sums[i, 17 + b * 8 : 25 + b * 8, :]
            part = flows_ref[i, here, :] * mid
            grad = part if grad is None else grad + part
        grad = turned(fixed[9, at, :] * grad * (1.0 / (NTM * STEPS)), 16, 1)
        gain = gains(at)
        scale = (None, 1.0 / fixed[6, at, :], 1.0 / fixed[7, at, :])

        def end(k, f):
            value = state[k, f, at, :]
            return value if f == 0 else value * scale[f]

        now = [end(NTM - 1, f) for f in range(3)]
        for k in range(NTM):
            if k > 0:
                now = [(end(k - 1, f) - old[k - 1, f, at, :]) + gain[f] * now[f] for f in range(3)]
            a, p, q = (turned(now[0], -16, 1), turned(now[1], 80, 1), turned(now[2], 48, 1))
            out_ref[k, here, 0:128] = jnp.where(lane < 96, a, p)
            out_ref[k, here, 128:256] = jnp.where(lane < 64, p, q)
            out_ref[k, here, 256:384] = jnp.where(lane < 32, q, grad)


def unpack_kernel(got_ref, state_ref, grad_ref):
    lane = lanes((8, COLS))
    for b in range(ROWS // 8):
        y = 0 if b < OROWS // 8 else 1
        at = slice(b * 8 - 64 * y, b * 8 - 64 * y + 8)
        here = slice(b * 8, b * 8 + 8)
        parts = [got_ref[y * 4 + x, at, :] for x in range(4)]
        for f in range(4):
            value = turned(parts[0], -CHUNK * f, 1)
            for x in range(1, 4):
                value = jnp.where(lane >= CHUNK * x, turned(parts[x], CHUNK * (x - f), 1), value)
            if f < 3:
                state_ref[f, here, :] = value
            else:
                grad_ref[here, :] = value


def waves():
    count = np.arange(1, NTM * STEPS + 1, dtype=np.float32)
    angle = np.float32(2.0 * math.pi) * count / np.float32(NTM * STEPS)
    return np.stack([np.cos(angle), np.sin(angle)]).astype(np.float32)


def shards(depth_class, ocean_mask, depth_levels, drag, tide_force, forward_flow, guess):
    guess = guess[0]
    lat, lat_size = (lax.axis_index("lat"), lax.axis_size("lat"))
    lat = jnp.reshape(lat, (1,)).astype(jnp.int32)
    k = jnp.reshape(lax.axis_index("tm"), (1,)).astype(jnp.int32)
    wave = jnp.asarray(waves())
    block = (ROWS, COLS)
    strip = (8, HALO, COLS)
    side = (ROWS, 256)
    ground, low, high, west, east = call(
        functools.partial(first_kernel, lat_size),
        ((2, *block), strip, strip, side, side),
        [
            pltpu.SMEM((32,), F32),
            pltpu.VMEM(block, jnp.int32),
            pltpu.VMEM(block, jnp.int32),
            pltpu.VMEM(block, F32),
            pltpu.VMEM((2, *block), F32),
            pltpu.VMEM((3, *block), F32),
            pltpu.SemaphoreType.DMA((6,)),
        ],
        [SMEM] + [pl.BlockSpec(memory_space=pltpu.HBM)] * 6,
        60,
    )(lat, depth_levels, depth_class, ocean_mask, drag, tide_force, guess)
    up = [(i, i + 1) for i in range(lat_size - 1)]
    down = [(i + 1, i) for i in range(lat_size - 1)]
    lon_size = lax.axis_size("lon")
    from_west = lax.ppermute(east, "lon", [(i, (i + 1) % lon_size) for i in range(lon_size)])
    from_east = lax.ppermute(west, "lon", [((i + 1) % lon_size, i) for i in range(lon_size)])
    from_south = lax.ppermute(high, "lat", up)
    from_north = lax.ppermute(low, "lat", down)
    fields = (ground, drag, tide_force, guess)
    inner_fixed, inner = call(
        interior_kernel,
        ((10, EROWS, COLS), (3, EROWS, COLS)),
        [pltpu.VMEM((8, EROWS, COLS), F32), pltpu.VMEM((3, EROWS, COLS), F32)],
        [SMEM, SMEM] + [VMEM] * 6,
        8,
        FLOPS,
    )(k, wave, *fields, from_south, from_north)
    to_north = jnp.concatenate([from_west[ROWS - HALO :], from_east[ROWS - HALO :]])
    to_south = jnp.concatenate([from_west[:HALO], from_east[:HALO]])
    corner_south = lax.ppermute(to_north, "lat", up)
    corner_north = lax.ppermute(to_south, "lat", down)
    sent, fixed, flows = call(
        edge_kernel,
        ((NTM, 3 * CROWS, 128), (10, CROWS, 128), (4, OROWS, 128)),
        [
            pltpu.VMEM((8, EROWS, 128), F32),
            pltpu.VMEM((10, EROWS, 128), F32),
            pltpu.VMEM((3, EROWS, 128), F32),
            pltpu.VMEM((3, EROWS, 128), F32),
        ],
        [SMEM, SMEM] + [VMEM] * 13,
        8,
    )(
        k, wave, *fields, forward_flow, from_south, from_north, from_west, from_east,
        corner_south, corner_north, inner_fixed, inner,
    )
    got = lax.all_to_all(sent, "tm", 0, 0, tiled=True)
    (back,) = call(
        last_kernel,
        ((NTM, OROWS, COLS),),
        [
            pltpu.VMEM((NTM, 3, CROWS, 128), F32),
            pltpu.VMEM((NTM, 3, CROWS, 128), F32),
            pltpu.VMEM((4, CROWS, 128), F32),
        ],
        [SMEM] + [VMEM] * 3,
        10,
    )(wave, got, fixed, flows)
    home = lax.all_to_all(back, "tm", 0, 0, tiled=True)
    state, grad = call(unpack_kernel, ((3, *block), block), [], [VMEM], 6)(home)
    return (state[None], grad)


def solution(mesh):
    return jax.shard_map(
        shards,
        mesh=mesh,
        in_specs=(
            P("lat", "lon"),
            P("lat", "lon"),
            P(),
            P("lat", "lon"),
            P(None, "lat", "lon"),
            P(None, "lat", "lon"),
            P("tm", None, "lat", "lon"),
        ),
        out_specs=(P("tm", None, "lat", "lon"), P("lat", "lon")),
        check_vma=False,
    )
```

```python
import functools
import math

import jax
import jax.numpy as jnp
import numpy as np
from jax import lax
from jax.experimental import pallas as pl
from jax.experimental.pallas import tpu as pltpu
from jax.sharding import PartitionSpec as P

STEPS = 16
NTM = 8
ROWS = 136
COLS = 384
HALO = 32
EROWS = ROWS + 2 * HALO
NB = EROWS // 8
CROWS = 104
CB = CROWS // 8
OROWS = 72
CHUNK = 96
VMEM = pl.BlockSpec(memory_space=pltpu.VMEM)
SMEM = pl.BlockSpec(memory_space=pltpu.SMEM)
F32 = jnp.float32
FLOPS = 30_000_000
SPLIT = 9


def lanes(shape):
    return lax.broadcasted_iota(jnp.int32, shape, 1)


def rows_of(shape):
    return lax.broadcasted_iota(jnp.int32, shape, 0)


def turned(value, shift, axis):
    size = value.shape[axis]
    shift = shift % size
    return value if shift == 0 else pltpu.roll(value, shift, axis)


def call(kernel, out_shapes, scratch, specs, mib, flops=0):
    outs = tuple(jax.ShapeDtypeStruct(s, F32) for s in out_shapes)
    cost = pl.CostEstimate(flops=flops, bytes_accessed=flops // 4, transcendentals=0) if flops else None
    return pl.pallas_call(
        kernel,
        out_shape=outs,
        in_specs=specs,
        out_specs=tuple(VMEM for _ in outs),
        scratch_shapes=scratch,
        cost_estimate=cost,
        compiler_params=pltpu.CompilerParams(vmem_limit_bytes=mib * 1024 * 1024),
    )


def first_kernel(
    lat_size, lat_ref, levels_hbm, cls_hbm, ocean_hbm, drag_hbm, force_hbm, guess_hbm,
    ground_ref, low_ref, high_ref, west_ref, east_ref,
    levels, cls_ref, ocean_ref, drag_ref, force_ref, guess_ref, sems,
):
    pairs = (
        (levels_hbm, levels), (cls_hbm, cls_ref), (ocean_hbm, ocean_ref),
        (drag_hbm, drag_ref), (force_hbm, force_ref), (guess_hbm, guess_ref),
    )
    copies = [pltpu.make_async_copy(src, dst, sems.at[i]) for i, (src, dst) in enumerate(pairs)]
    for copy in copies:
        copy.start()
    for copy in copies[:3]:
        copy.wait()
    level = [levels[i] for i in range(32)]
    lat = lat_ref[0]
    first = jnp.where(lat == 0, 0, -1)
    last = jnp.where(lat == lat_size - 1, ROWS - 1, -1)
    for b in range(ROWS // 8):
        at = slice(b * 8, b * 8 + 8)
        cls = cls_ref[at, :]
        row = rows_of(cls.shape) + b * 8
        vals = level
        for bit in range(5):
            odd = (cls & (1 << bit)) != 0
            vals = [jnp.where(odd, vals[2 * i + 1], vals[2 * i]) for i in range(len(vals) // 2)]
        ground_ref[0, at, :] = vals[0]
        polar = (row == first) | (row == last)
        ground_ref[1, at, :] = jnp.where(polar, 0.0, ocean_ref[at, :].astype(F32))
    for copy in copies[3:]:
        copy.wait()
    own = own_fields(ground_ref, drag_ref, force_ref, guess_ref)
    for out, start in ((low_ref, 0), (high_ref, ROWS - HALO)):
        for f in range(8):
            out[f] = own[f][start : start + HALO, :]
    lane = lanes((ROWS, 128))
    for out, tile, base in ((west_ref, 0, 0), (east_ref, COLS - 128, 96)):
        for half in range(2):
            packed = None
            for j in range(4):
                piece = turned(own[half * 4 + j][:, tile : tile + 128], j * 32 - base, 1)
                packed = piece if j == 0 else jnp.where(lane >= j * 32, piece, packed)
            out[:, half * 128 : half * 128 + 128] = packed


def own_fields(ground_ref, drag_ref, force_ref, guess_ref):
    views = [ground_ref.at[0], ground_ref.at[1], drag_ref, force_ref.at[0], force_ref.at[1]]
    return views + [guess_ref.at[f] for f in range(3)]


def south(block, before, row):
    return jnp.where(row == 0, turned(before, 1, 0), turned(block, 1, 0))


def power16(x):
    for _ in range(4):
        x = x * x
    return x


def prepare(raw, fixed, gone, flux, keepf, row):
    def band(b, carry):
        at = pl.ds(pl.multiple_of(b * 8, 8), 8)
        up = pl.ds(pl.multiple_of(lax.rem(b + NB - 1, NB) * 8, 8), 8)

        def pair(f):
            x = raw[f, at, :]
            before = raw[f, up, :]
            if f == 0:
                x = jnp.where(x > 0.0, x, 1.0)
                before = jnp.where(before > 0.0, before, 1.0)
            return x, turned(x, 1, 1), south(x, before, row)

        dep, dep_w, dep_s = pair(0)
        m, m_w, m_s = pair(1)
        dr, dr_w, dr_s = pair(2)
        mu, mv = (m * m_w, m * m_s)
        mdu = mu * (1.0 - (dr + dr_w) / (dep + dep_w))
        mdv = mv * (1.0 - (dr + dr_s) / (dep + dep_s))
        hu, hv = (0.3 * (dep + dep_w), 0.3 * (dep + dep_s))
        fixed[0, at, :] = mdu
        fixed[1, at, :] = (0.7 * mu) * hu
        fixed[2, at, :] = mdv
        fixed[3, at, :] = (0.7 * mv) * hv
        fixed[4, at, :] = m * raw[3, at, :]
        fixed[5, at, :] = m * raw[4, at, :]
        fixed[6, at, :] = hu
        fixed[7, at, :] = hv
        fixed[8, at, :] = m
        fixed[9, at, :] = 0.5 * m / dep
        elev, zonal, merid = (m * raw[5, at, :], raw[6, at, :], raw[7, at, :])
        flux[0, at, :] = elev
        flux[1, at, :] = hu * zonal
        flux[2, at, :] = hv * merid
        gone[0, at, :] = keepf * elev
        gone[1, at, :] = keepf * (power16(mdu) * zonal)
        gone[2, at, :] = keepf * (power16(mdv) * merid)
        return carry

    lax.fori_loop(0, NB, band, 0, unroll=5)


def fine(fixed, flux, wave_ref, k, row, first, last):
    def step(s, carry):
        c, z = (wave_ref[0, k * STEPS + s], wave_ref[1, k * STEPS + s])
        a = flux[0, EROWS - 8 :, :]
        turned_a = turned(a, 1, 0)
        after = jnp.zeros(a.shape, F32)
        for b in range(NB - 1, -1, -1):
            at = slice(b * 8, b * 8 + 8)
            a_before = flux[0, b * 8 - 8 : b * 8, :] if b > 0 else a
            turned_before = turned(a_before, 1, 0) if b > 0 else turned_a
            a_s = jnp.where(row == 0, turned_before, turned_a)
            u = fixed[0, at, :] * flux[1, at, :] - fixed[1, at, :] * (a - turned(a, 1, 1))
            v = fixed[2, at, :] * flux[2, at, :] - fixed[3, at, :] * (a - a_s)
            flux[1, at, :] = u
            flux[2, at, :] = v
            turned_v = turned(v, -1, 0)
            v_n = jnp.where(row == 7, after, turned_v)
            source = fixed[4, at, :] * c + fixed[5, at, :] * z
            flux[0, at, :] = (a + source) - ((turned(u, -1, 1) - u) + (v_n - v))
            a, turned_a, after = (a_before, turned_before, turned_v)
        return carry

    lax.fori_loop(first, last, step, 0)


def finish(fixed, flux, gone):
    for b in range(2, NB - 2):
        at = slice(b * 8, b * 8 + 8)
        flux[0, at, :] = flux[0, at, :] - gone[0, at, :]
        flux[1, at, :] = flux[1, at, :] / fixed[6, at, :] - gone[1, at, :]
        flux[2, at, :] = flux[2, at, :] / fixed[7, at, :] - gone[2, at, :]


def interior_kernel(
    k_ref, wave_ref, ground_ref, drag_ref, force_ref, guess_ref, south_ref, north_ref, fixed, flux, gone, raw,
):
    own = own_fields(ground_ref, drag_ref, force_ref, guess_ref)
    k = k_ref[0]
    for f in range(8):
        raw[f, 0:HALO, :] = south_ref[f]
        raw[f, HALO : HALO + ROWS, :] = own[f][...]
        raw[f, HALO + ROWS :, :] = north_ref[f]
    row = rows_of((8, COLS))
    prepare(raw, fixed, gone, flux, jnp.where(k == NTM - 1, 0.0, 1.0), row)
    fine(fixed, flux, wave_ref, k, row, 0, SPLIT)


def second_kernel(k_ref, wave_ref, fixed, before, gone, flux):
    for f in range(3):
        flux[f] = before[f]
    fine(fixed, flux, wave_ref, k_ref[0], rows_of((8, COLS)), SPLIT, STEPS)
    finish(fixed, flux, gone)


def shifted_tiles(left, right, start):
    return jnp.where(lanes(left.shape) < 128 - start, turned(left, -start, 1), turned(right, -start, 1))


def chunk_tile(inner, edge, x):
    if x == 0:
        first = edge()
        return jnp.where(lanes(first.shape) < 32, turned(first, -16, 1), turned(inner(0), 16, 1))
    if x == 3:
        first = edge()
        return jnp.where(lanes(first.shape) >= 96, turned(first, 16, 1), turned(inner(2), -16, 1))
    return shifted_tiles(inner(x - 1), inner(x), 96 * x - 16 - 128 * (x - 1))


def edge_kernel(
    k_ref, wave_ref, ground_ref, drag_ref, force_ref, guess_ref, flow_ref, south_ref, north_ref,
    from_west, from_east, corner_south, corner_north, inner_fixed, inner,
    out_ref, fixed_ref, flows_ref, raw, fixed, gone, flux,
):
    own = own_fields(ground_ref, drag_ref, force_ref, guess_ref)
    k = k_ref[0]
    cy, cx = (lax.shift_right_logical(k, 2), k & 3)
    for f in range(8):
        j, at = (f % 4, slice(f // 4 * 128, f // 4 * 128 + 128))
        parts = (
            (0, HALO, south_ref.at[f], corner_south[0:HALO, at], corner_south[HALO:, at]),
            (HALO, ROWS, own[f], from_west[:, at], from_east[:, at]),
            (HALO + ROWS, HALO, north_ref.at[f], corner_north[0:HALO, at], corner_north[HALO:, at]),
        )
        for start, size, mine, west, east in parts:
            lane = lanes((size, 128))
            low = jnp.where(lane < 32, turned(west, -j * 32, 1), turned(mine[:, 0:128], 32, 1))
            high = jnp.where(lane >= 96, turned(east, 96 - j * 32, 1), turned(mine[:, COLS - 128 :], -32, 1))
            raw[f, start : start + size, :] = jnp.where(lane < 64, low, high)
    row = rows_of((8, 128))
    prepare(raw, fixed, gone, flux, jnp.where(k == NTM - 1, 0.0, 1.0), row)
    fine(fixed, flux, wave_ref, k, row, 0, STEPS)
    finish(fixed, flux, gone)

    for y in range(2):
        at = slice(16 + 64 * y, 16 + 64 * y + CROWS)
        for f in range(3):
            for x in range(4):
                tile = chunk_tile(
                    lambda t: inner[f, at, t * 128 : t * 128 + 128], lambda: flux[f, at, :], x
                )
                out_ref[y * 4 + x, f * CROWS : (f + 1) * CROWS, :] = tile

    top = pl.ds(pl.multiple_of(16 + 64 * cy, 8), CROWS)
    mid = pl.ds(pl.multiple_of(64 * cy, 8), OROWS)
    for x in range(4):

        @pl.when(cx == x)
        def _(x=x):
            for f in range(10):
                fixed_ref[f] = chunk_tile(
                    lambda t: inner_fixed[f, top, t * 128 : t * 128 + 128], lambda: fixed[f, top, :], x
                )
            for f in range(4):
                view = lambda t: flow_ref[f, mid, t * 128 : t * 128 + 128]
                if x == 0:
                    flows_ref[f] = turned(view(0), 16, 1)
                elif x == 3:
                    flows_ref[f] = turned(view(2), -16, 1)
                else:
                    flows_ref[f] = chunk_tile(view, None, x)


def last_kernel(wave_ref, got_ref, fixed, flows_ref, out_ref, state, old, sums):
    row = rows_of((8, 128))

    def gains(at):
        return (fixed[8, at, :], power16(fixed[0, at, :]), power16(fixed[2, at, :]))

    def start(b, carry):
        at = pl.ds(pl.multiple_of(b * 8, 8), 8)
        gain = gains(at)
        scale = (None, fixed[6, at, :], fixed[7, at, :])
        for f in range(3):
            line = pl.ds(pl.multiple_of(f * CROWS + b * 8, 8), 8)
            now = got_ref[NTM - 1, line, :]
            for k in range(NTM):
                if k > 0:
                    now = got_ref[k - 1, line, :] + gain[f] * now
                state[k, f, at, :] = now if f == 0 else scale[f] * now
                old[k, f, at, :] = gain[f] * now
        return carry

    lax.fori_loop(0, CB, start, 0)
    for i in range(4):
        sums[i] = jnp.zeros((CROWS, 128), F32)
    half = math.sqrt(0.5)

    def step(s, carry):
        c, z = (wave_ref[0, s], wave_ref[1, s])
        for b in range(CB - 1, -1, -1):
            at = slice(b * 8, b * 8 + 8)
            mdu, ku, mdv, kv, f0, f1 = [fixed[i, at, :] for i in range(6)]
            even, odd = (f0 * c + f1 * z, f1 * c - f0 * z)
            source = (even, half * (odd + even), odd, half * (odd - even))
            split = ([None] * NTM, [None] * NTM)
            for k in (0, 4, 1, 5, 2, 6, 3, 7):
                a = state[k, 0, at, :]
                a_s = state[k, 0, b * 8 - 1 : b * 8 + 7, :] if b > 0 else turned(a, 1, 0)
                u = mdu * state[k, 1, at, :] - ku * (a - turned(a, 1, 1))
                v = mdv * state[k, 2, at, :] - kv * (a - a_s)
                state[k, 1, at, :] = u
                state[k, 2, at, :] = v
                v_n = state[k, 2, b * 8 + 1 : b * 8 + 9, :] if b < CB - 1 else turned(v, -1, 0)
                forced = a + source[k] if k < 4 else a - source[k - 4]
                state[k, 0, at, :] = forced - ((turned(u, -1, 1) - u) + (v_n - v))
                for part, value in zip(split, (u, v)):
                    if k < 4:
                        part[k] = value
                    else:
                        part[k - 4] = part[k - 4] - value
            if 2 <= b <= 11:
                for i in range(2):
                    w = split[i]
                    x = w[0] + half * (w[1] - w[3])
                    y = w[2] + half * (w[1] + w[3])
                    sums[2 * i, at, :] = sums[2 * i, at, :] + (c * x - z * y)
                    sums[2 * i + 1, at, :] = sums[2 * i + 1, at, :] + (z * x + c * y)
        return carry

    lax.fori_loop(0, STEPS, step, 0)
    for b in range(2, 12):
        at = slice(b * 8, b * 8 + 8)
        for i in range(4):
            sums[i, at, :] = sums[i, at, :] / fixed[6 + i // 2, at, :]

    lane = lanes((8, 128))
    for b in range(OROWS // 8):
        at = slice(16 + b * 8, 24 + b * 8)
        here = slice(b * 8, b * 8 + 8)
        grad = None
        for i in range(4):
            x = sums[i, at, :]
            if i < 2:
                mid = x + turned(x, -1, 1)
            else:
                mid = x + sums[i, 17 + b * 8 : 25 + b * 8, :]
            part = flows_ref[i, here, :] * mid
            grad = part if grad is None else grad + part
        grad = turned(fixed[9, at, :] * grad * (1.0 / (NTM * STEPS)), 16, 1)
        gain = gains(at)
        scale = (None, 1.0 / fixed[6, at, :], 1.0 / fixed[7, at, :])

        def end(k, f):
            value = state[k, f, at, :]
            return value if f == 0 else value * scale[f]

        now = [end(NTM - 1, f) for f in range(3)]
        for k in range(NTM):
            if k > 0:
                now = [(end(k - 1, f) - old[k - 1, f, at, :]) + gain[f] * now[f] for f in range(3)]
            a, p, q = (turned(now[0], -16, 1), turned(now[1], 80, 1), turned(now[2], 48, 1))
            out_ref[k, here, 0:128] = jnp.where(lane < 96, a, p)
            out_ref[k, here, 128:256] = jnp.where(lane < 64, p, q)
            out_ref[k, here, 256:384] = jnp.where(lane < 32, q, grad)


def unpack_kernel(got_ref, state_ref, grad_ref):
    lane = lanes((8, COLS))
    for b in range(ROWS // 8):
        y = 0 if b < OROWS // 8 else 1
        at = slice(b * 8 - 64 * y, b * 8 - 64 * y + 8)
        here = slice(b * 8, b * 8 + 8)
        parts = [got_ref[y * 4 + x, at, :] for x in range(4)]
        for f in range(4):
            value = turned(parts[0], -CHUNK * f, 1)
            for x in range(1, 4):
                value = jnp.where(lane >= CHUNK * x, turned(parts[x], CHUNK * (x - f), 1), value)
            if f < 3:
                state_ref[f, here, :] = value
            else:
                grad_ref[here, :] = value


def waves():
    count = np.arange(1, NTM * STEPS + 1, dtype=np.float32)
    angle = np.float32(2.0 * math.pi) * count / np.float32(NTM * STEPS)
    return np.stack([np.cos(angle), np.sin(angle)]).astype(np.float32)


def shards(depth_class, ocean_mask, depth_levels, drag, tide_force, forward_flow, guess):
    guess = guess[0]
    lat, lat_size = (lax.axis_index("lat"), lax.axis_size("lat"))
    lat = jnp.reshape(lat, (1,)).astype(jnp.int32)
    k = jnp.reshape(lax.axis_index("tm"), (1,)).astype(jnp.int32)
    wave = jnp.asarray(waves())
    block = (ROWS, COLS)
    strip = (8, HALO, COLS)
    side = (ROWS, 256)
    ground, low, high, west, east = call(
        functools.partial(first_kernel, lat_size),
        ((2, *block), strip, strip, side, side),
        [
            pltpu.SMEM((32,), F32),
            pltpu.VMEM(block, jnp.int32),
            pltpu.VMEM(block, jnp.int32),
            pltpu.VMEM(block, F32),
            pltpu.VMEM((2, *block), F32),
            pltpu.VMEM((3, *block), F32),
            pltpu.SemaphoreType.DMA((6,)),
        ],
        [SMEM] + [pl.BlockSpec(memory_space=pltpu.HBM)] * 6,
        60,
    )(lat, depth_levels, depth_class, ocean_mask, drag, tide_force, guess)
    up = [(i, i + 1) for i in range(lat_size - 1)]
    down = [(i + 1, i) for i in range(lat_size - 1)]
    lon_size = lax.axis_size("lon")
    from_west = lax.ppermute(east, "lon", [(i, (i + 1) % lon_size) for i in range(lon_size)])
    from_east = lax.ppermute(west, "lon", [((i + 1) % lon_size, i) for i in range(lon_size)])
    from_south = lax.ppermute(high, "lat", up)
    from_north = lax.ppermute(low, "lat", down)
    fields = (ground, drag, tide_force, guess)
    deep = (3, EROWS, COLS)
    inner_fixed, half, gone = call(
        interior_kernel,
        ((10, EROWS, COLS), deep, deep),
        [pltpu.VMEM((8, EROWS, COLS), F32)],
        [SMEM, SMEM] + [VMEM] * 6,
        8,
        FLOPS,
    )(k, wave, *fields, from_south, from_north)
    from_west, from_east, half = lax.optimization_barrier((from_west, from_east, half))
    (inner,) = call(second_kernel, (deep,), [], [SMEM, SMEM] + [VMEM] * 3, 4, FLOPS)(
        k, wave, inner_fixed, half, gone
    )
    to_north = jnp.concatenate([from_west[ROWS - HALO :], from_east[ROWS - HALO :]])
    to_south = jnp.concatenate([from_west[:HALO], from_east[:HALO]])
    corner_south = lax.ppermute(to_north, "lat", up)
    corner_north = lax.ppermute(to_south, "lat", down)
    sent, fixed, flows = call(
        edge_kernel,
        ((NTM, 3 * CROWS, 128), (10, CROWS, 128), (4, OROWS, 128)),
        [
            pltpu.VMEM((8, EROWS, 128), F32),
            pltpu.VMEM((10, EROWS, 128), F32),
            pltpu.VMEM((3, EROWS, 128), F32),
            pltpu.VMEM((3, EROWS, 128), F32),
        ],
        [SMEM, SMEM] + [VMEM] * 13,
        8,
    )(
        k, wave, *fields, forward_flow, from_south, from_north, from_west, from_east,
        corner_south, corner_north, inner_fixed, inner,
    )
    got = lax.all_to_all(sent, "tm", 0, 0, tiled=True)
    (back,) = call(
        last_kernel,
        ((NTM, OROWS, COLS),),
        [
            pltpu.VMEM((NTM, 3, CROWS, 128), F32),
            pltpu.VMEM((NTM, 3, CROWS, 128), F32),
            pltpu.VMEM((4, CROWS, 128), F32),
        ],
        [SMEM] + [VMEM] * 3,
        10,
    )(wave, got, fixed, flows)
    home = lax.all_to_all(back, "tm", 0, 0, tiled=True)
    state, grad = call(unpack_kernel, ((3, *block), block), [], [VMEM], 6)(home)
    return (state[None], grad)


def solution(mesh):
    return jax.shard_map(
        shards,
        mesh=mesh,
        in_specs=(
            P("lat", "lon"),
            P("lat", "lon"),
            P(),
            P("lat", "lon"),
            P(None, "lat", "lon"),
            P(None, "lat", "lon"),
            P("tm", None, "lat", "lon"),
        ),
        out_specs=(P("tm", None, "lat", "lon"), P("lat", "lon")),
        check_vma=False,
    )
```

```python
import functools
import math

import jax
import jax.numpy as jnp
import numpy as np
from jax import lax
from jax.experimental import pallas as pl
from jax.experimental.pallas import tpu as pltpu
from jax.sharding import PartitionSpec as P

STEPS = 16
NTM = 8
ROWS = 136
COLS = 384
HALO = 32
EROWS = ROWS + 2 * HALO
NB = EROWS // 8
CROWS = 104
CB = CROWS // 8
OROWS = 72
CHUNK = 96
VMEM = pl.BlockSpec(memory_space=pltpu.VMEM)
SMEM = pl.BlockSpec(memory_space=pltpu.SMEM)
F32 = jnp.float32
FLOPS = 30_000_000
SPLIT = 9


def lanes(shape):
    return lax.broadcasted_iota(jnp.int32, shape, 1)


def rows_of(shape):
    return lax.broadcasted_iota(jnp.int32, shape, 0)


def turned(value, shift, axis):
    size = value.shape[axis]
    shift = shift % size
    return value if shift == 0 else pltpu.roll(value, shift, axis)


def call(kernel, out_shapes, scratch, specs, mib, flops=0):
    outs = tuple(jax.ShapeDtypeStruct(s, F32) for s in out_shapes)
    cost = pl.CostEstimate(flops=flops, bytes_accessed=flops // 4, transcendentals=0) if flops else None
    return pl.pallas_call(
        kernel,
        out_shape=outs,
        in_specs=specs,
        out_specs=tuple(VMEM for _ in outs),
        scratch_shapes=scratch,
        cost_estimate=cost,
        compiler_params=pltpu.CompilerParams(vmem_limit_bytes=mib * 1024 * 1024),
    )


def first_kernel(
    lat_size, lat_ref, levels_hbm, cls_hbm, ocean_hbm, drag_hbm, force_hbm, guess_hbm,
    ground_ref, low_ref, high_ref, west_ref, east_ref,
    levels, cls_ref, ocean_ref, drag_ref, force_ref, guess_ref, sems,
):
    pairs = (
        (levels_hbm, levels), (cls_hbm, cls_ref), (ocean_hbm, ocean_ref),
        (drag_hbm, drag_ref), (force_hbm, force_ref), (guess_hbm, guess_ref),
    )
    copies = [pltpu.make_async_copy(src, dst, sems.at[i]) for i, (src, dst) in enumerate(pairs)]
    for copy in copies:
        copy.start()
    for copy in copies[:3]:
        copy.wait()
    level = [levels[i] for i in range(32)]
    lat = lat_ref[0]
    first = jnp.where(lat == 0, 0, -1)
    last = jnp.where(lat == lat_size - 1, ROWS - 1, -1)
    for b in range(ROWS // 8):
        at = slice(b * 8, b * 8 + 8)
        cls = cls_ref[at, :]
        row = rows_of(cls.shape) + b * 8
        vals = level
        for bit in range(5):
            odd = (cls & (1 << bit)) != 0
            vals = [jnp.where(odd, vals[2 * i + 1], vals[2 * i]) for i in range(len(vals) // 2)]
        ground_ref[0, at, :] = vals[0]
        polar = (row == first) | (row == last)
        ground_ref[1, at, :] = jnp.where(polar, 0.0, ocean_ref[at, :].astype(F32))
    for copy in copies[3:]:
        copy.wait()
    own = own_fields(ground_ref, drag_ref, force_ref, guess_ref)
    for out, start in ((low_ref, 0), (high_ref, ROWS - HALO)):
        for f in range(8):
            out[f] = own[f][start : start + HALO, :]
    lane = lanes((ROWS, 128))
    for out, tile, base in ((west_ref, 0, 0), (east_ref, COLS - 128, 96)):
        for half in range(2):
            packed = None
            for j in range(4):
                piece = turned(own[half * 4 + j][:, tile : tile + 128], j * 32 - base, 1)
                packed = piece if j == 0 else jnp.where(lane >= j * 32, piece, packed)
            out[:, half * 128 : half * 128 + 128] = packed


def own_fields(ground_ref, drag_ref, force_ref, guess_ref):
    views = [ground_ref.at[0], ground_ref.at[1], drag_ref, force_ref.at[0], force_ref.at[1]]
    return views + [guess_ref.at[f] for f in range(3)]


def south(block, before, row):
    return jnp.where(row == 0, turned(before, 1, 0), turned(block, 1, 0))


def power16(x):
    for _ in range(4):
        x = x * x
    return x


def prepare(raw, fixed, gone, flux, keepf, row):
    def band(b, carry):
        at = pl.ds(pl.multiple_of(b * 8, 8), 8)
        up = pl.ds(pl.multiple_of(lax.rem(b + NB - 1, NB) * 8, 8), 8)

        def pair(f):
            x = raw[f, at, :]
            before = raw[f, up, :]
            if f == 0:
                x = jnp.where(x > 0.0, x, 1.0)
                before = jnp.where(before > 0.0, before, 1.0)
            return x, turned(x, 1, 1), south(x, before, row)

        dep, dep_w, dep_s = pair(0)
        m, m_w, m_s = pair(1)
        dr, dr_w, dr_s = pair(2)
        mu, mv = (m * m_w, m * m_s)
        mdu = mu * (1.0 - (dr + dr_w) / (dep + dep_w))
        mdv = mv * (1.0 - (dr + dr_s) / (dep + dep_s))
        hu, hv = (0.3 * (dep + dep_w), 0.3 * (dep + dep_s))
        fixed[0, at, :] = mdu
        fixed[1, at, :] = (0.7 * mu) * hu
        fixed[2, at, :] = mdv
        fixed[3, at, :] = (0.7 * mv) * hv
        fixed[4, at, :] = m * raw[3, at, :]
        fixed[5, at, :] = m * raw[4, at, :]
        fixed[6, at, :] = hu
        fixed[7, at, :] = hv
        fixed[8, at, :] = m
        fixed[9, at, :] = 0.5 * m / dep
        elev, zonal, merid = (m * raw[5, at, :], raw[6, at, :], raw[7, at, :])
        flux[0, at, :] = elev
        flux[1, at, :] = hu * zonal
        flux[2, at, :] = hv * merid
        gone[0, at, :] = keepf * elev
        gone[1, at, :] = keepf * (power16(mdu) * zonal)
        gone[2, at, :] = keepf * (power16(mdv) * merid)
        return carry

    lax.fori_loop(0, NB, band, 0, unroll=5)


def fine(fixed, flux, wave_ref, k, row, first, last):
    def step(s, carry):
        c, z = (wave_ref[0, k * STEPS + s], wave_ref[1, k * STEPS + s])
        a = flux[0, EROWS - 8 :, :]
        turned_a = turned(a, 1, 0)
        after = jnp.zeros(a.shape, F32)
        for b in range(NB - 1, -1, -1):
            at = slice(b * 8, b * 8 + 8)
            a_before = flux[0, b * 8 - 8 : b * 8, :] if b > 0 else a
            turned_before = turned(a_before, 1, 0) if b > 0 else turned_a
            a_s = jnp.where(row == 0, turned_before, turned_a)
            u = fixed[0, at, :] * flux[1, at, :] - fixed[1, at, :] * (a - turned(a, 1, 1))
            v = fixed[2, at, :] * flux[2, at, :] - fixed[3, at, :] * (a - a_s)
            flux[1, at, :] = u
            flux[2, at, :] = v
            turned_v = turned(v, -1, 0)
            v_n = jnp.where(row == 7, after, turned_v)
            source = fixed[4, at, :] * c + fixed[5, at, :] * z
            flux[0, at, :] = (a + source) - ((turned(u, -1, 1) - u) + (v_n - v))
            a, turned_a, after = (a_before, turned_before, turned_v)
        return carry

    lax.fori_loop(first, last, step, 0)


def finish(fixed, flux, gone):
    for b in range(2, NB - 2):
        at = slice(b * 8, b * 8 + 8)
        flux[0, at, :] = flux[0, at, :] - gone[0, at, :]
        flux[1, at, :] = flux[1, at, :] / fixed[6, at, :] - gone[1, at, :]
        flux[2, at, :] = flux[2, at, :] / fixed[7, at, :] - gone[2, at, :]


def interior_kernel(
    k_ref, wave_ref, ground_ref, drag_ref, force_ref, guess_ref, south_ref, north_ref, fixed, flux, gone, raw,
):
    own = own_fields(ground_ref, drag_ref, force_ref, guess_ref)
    k = k_ref[0]
    for f in range(8):
        raw[f, 0:HALO, :] = south_ref[f]
        raw[f, HALO : HALO + ROWS, :] = own[f][...]
        raw[f, HALO + ROWS :, :] = north_ref[f]
    row = rows_of((8, COLS))
    prepare(raw, fixed, gone, flux, jnp.where(k == NTM - 1, 0.0, 1.0), row)
    fine(fixed, flux, wave_ref, k, row, 0, SPLIT)


def second_kernel(k_ref, wave_ref, fixed, before, gone, flux):
    for f in range(3):
        flux[f] = before[f]
    fine(fixed, flux, wave_ref, k_ref[0], rows_of((8, COLS)), SPLIT, STEPS)
    finish(fixed, flux, gone)


def shifted_tiles(left, right, start):
    return jnp.where(lanes(left.shape) < 128 - start, turned(left, -start, 1), turned(right, -start, 1))


def chunk_tile(inner, edge, x):
    if x == 0:
        first = edge()
        return jnp.where(lanes(first.shape) < 32, turned(first, -16, 1), turned(inner(0), 16, 1))
    if x == 3:
        first = edge()
        return jnp.where(lanes(first.shape) >= 96, turned(first, 16, 1), turned(inner(2), -16, 1))
    return shifted_tiles(inner(x - 1), inner(x), 96 * x - 16 - 128 * (x - 1))


def edge_kernel(
    k_ref, wave_ref, ground_ref, drag_ref, force_ref, guess_ref, flow_ref, south_ref, north_ref,
    from_west, from_east, corner_south, corner_north, inner_fixed, inner,
    out_ref, fixed_ref, flows_ref, raw, fixed, gone, flux,
):
    own = own_fields(ground_ref, drag_ref, force_ref, guess_ref)
    k = k_ref[0]
    cy, cx = (lax.shift_right_logical(k, 2), k & 3)
    for f in range(8):
        j, at = (f % 4, slice(f // 4 * 128, f // 4 * 128 + 128))
        parts = (
            (0, HALO, south_ref.at[f], corner_south[0:HALO, at], corner_south[HALO:, at]),
            (HALO, ROWS, own[f], from_west[:, at], from_east[:, at]),
            (HALO + ROWS, HALO, north_ref.at[f], corner_north[0:HALO, at], corner_north[HALO:, at]),
        )
        for start, size, mine, west, east in parts:
            lane = lanes((size, 128))
            low = jnp.where(lane < 32, turned(west, -j * 32, 1), turned(mine[:, 0:128], 32, 1))
            high = jnp.where(lane >= 96, turned(east, 96 - j * 32, 1), turned(mine[:, COLS - 128 :], -32, 1))
            raw[f, start : start + size, :] = jnp.where(lane < 64, low, high)
    row = rows_of((8, 128))
    prepare(raw, fixed, gone, flux, jnp.where(k == NTM - 1, 0.0, 1.0), row)
    fine(fixed, flux, wave_ref, k, row, 0, STEPS)
    finish(fixed, flux, gone)

    for y in range(2):
        at = slice(16 + 64 * y, 16 + 64 * y + CROWS)
        for f in range(3):
            for x in range(4):
                tile = chunk_tile(
                    lambda t: inner[f, at, t * 128 : t * 128 + 128], lambda: flux[f, at, :], x
                )
                out_ref[y * 4 + x, f * CROWS : (f + 1) * CROWS, :] = tile

    top = pl.ds(pl.multiple_of(16 + 64 * cy, 8), CROWS)
    mid = pl.ds(pl.multiple_of(64 * cy, 8), OROWS)
    for x in range(4):

        @pl.when(cx == x)
        def _(x=x):
            for f in range(10):
                fixed_ref[f] = chunk_tile(
                    lambda t: inner_fixed[f, top, t * 128 : t * 128 + 128], lambda: fixed[f, top, :], x
                )
            for f in range(4):
                view = lambda t: flow_ref[f, mid, t * 128 : t * 128 + 128]
                if x == 0:
                    flows_ref[f] = turned(view(0), 16, 1)
                elif x == 3:
                    flows_ref[f] = turned(view(2), -16, 1)
                else:
                    flows_ref[f] = chunk_tile(view, None, x)


def last_kernel(wave_ref, got_ref, fixed, flows_ref, out_ref, state, old, sums):
    row = rows_of((8, 128))

    def gains(at):
        return (fixed[8, at, :], power16(fixed[0, at, :]), power16(fixed[2, at, :]))

    def start(b, carry):
        at = pl.ds(pl.multiple_of(b * 8, 8), 8)
        gain = gains(at)
        scale = (None, fixed[6, at, :], fixed[7, at, :])
        for f in range(3):
            line = pl.ds(pl.multiple_of(f * CROWS + b * 8, 8), 8)
            now = got_ref[NTM - 1, line, :]
            for k in range(NTM):
                if k > 0:
                    now = got_ref[k - 1, line, :] + gain[f] * now
                state[k, f, at, :] = now if f == 0 else scale[f] * now
                old[k, f, at, :] = gain[f] * now
        return carry

    lax.fori_loop(0, CB, start, 0, unroll=True)
    for i in range(4):
        sums[i] = jnp.zeros((CROWS, 128), F32)
    half = math.sqrt(0.5)

    def step(s, carry):
        c, z = (wave_ref[0, s], wave_ref[1, s])
        for b in range(CB - 1, -1, -1):
            at = slice(b * 8, b * 8 + 8)
            mdu, ku, mdv, kv, f0, f1 = [fixed[i, at, :] for i in range(6)]
            even, odd = (f0 * c + f1 * z, f1 * c - f0 * z)
            source = (even, half * (odd + even), odd, half * (odd - even))
            split = ([None] * NTM, [None] * NTM)
            for k in (0, 4, 1, 5, 2, 6, 3, 7):
                a = state[k, 0, at, :]
                a_s = state[k, 0, b * 8 - 1 : b * 8 + 7, :] if b > 0 else turned(a, 1, 0)
                u = mdu * state[k, 1, at, :] - ku * (a - turned(a, 1, 1))
                v = mdv * state[k, 2, at, :] - kv * (a - a_s)
                state[k, 1, at, :] = u
                state[k, 2, at, :] = v
                v_n = state[k, 2, b * 8 + 1 : b * 8 + 9, :] if b < CB - 1 else turned(v, -1, 0)
                forced = a + source[k] if k < 4 else a - source[k - 4]
                state[k, 0, at, :] = forced - ((turned(u, -1, 1) - u) + (v_n - v))
                for part, value in zip(split, (u, v)):
                    if k < 4:
                        part[k] = value
                    else:
                        part[k - 4] = part[k - 4] - value
            if 2 <= b <= 11:
                for i in range(2):
                    w = split[i]
                    x = w[0] + half * (w[1] - w[3])
                    y = w[2] + half * (w[1] + w[3])
                    sums[2 * i, at, :] = sums[2 * i, at, :] + (c * x - z * y)
                    sums[2 * i + 1, at, :] = sums[2 * i + 1, at, :] + (z * x + c * y)
        return carry

    lax.fori_loop(0, STEPS, step, 0)
    for b in range(2, 12):
        at = slice(b * 8, b * 8 + 8)
        for i in range(4):
            sums[i, at, :] = sums[i, at, :] / fixed[6 + i // 2, at, :]

    lane = lanes((8, 128))
    for b in range(OROWS // 8):
        at = slice(16 + b * 8, 24 + b * 8)
        here = slice(b * 8, b * 8 + 8)
        grad = None
        for i in range(4):
            x = sums[i, at, :]
            if i < 2:
                mid = x + turned(x, -1, 1)
            else:
                mid = x + sums[i, 17 + b * 8 : 25 + b * 8, :]
            part = flows_ref[i, here, :] * mid
            grad = part if grad is None else grad + part
        grad = turned(fixed[9, at, :] * grad * (1.0 / (NTM * STEPS)), 16, 1)
        gain = gains(at)
        scale = (None, 1.0 / fixed[6, at, :], 1.0 / fixed[7, at, :])

        def end(k, f):
            value = state[k, f, at, :]
            return value if f == 0 else value * scale[f]

        now = [end(NTM - 1, f) for f in range(3)]
        for k in range(NTM):
            if k > 0:
                now = [(end(k - 1, f) - old[k - 1, f, at, :]) + gain[f] * now[f] for f in range(3)]
            a, p, q = (turned(now[0], -16, 1), turned(now[1], 80, 1), turned(now[2], 48, 1))
            out_ref[k, here, 0:128] = jnp.where(lane < 96, a, p)
            out_ref[k, here, 128:256] = jnp.where(lane < 64, p, q)
            out_ref[k, here, 256:384] = jnp.where(lane < 32, q, grad)


def unpack_kernel(got_ref, state_ref, grad_ref):
    lane = lanes((8, COLS))
    for b in range(ROWS // 8):
        y = 0 if b < OROWS // 8 else 1
        at = slice(b * 8 - 64 * y, b * 8 - 64 * y + 8)
        here = slice(b * 8, b * 8 + 8)
        parts = [got_ref[y * 4 + x, at, :] for x in range(4)]
        for f in range(4):
            value = turned(parts[0], -CHUNK * f, 1)
            for x in range(1, 4):
                value = jnp.where(lane >= CHUNK * x, turned(parts[x], CHUNK * (x - f), 1), value)
            if f < 3:
                state_ref[f, here, :] = value
            else:
                grad_ref[here, :] = value


def waves():
    count = np.arange(1, NTM * STEPS + 1, dtype=np.float32)
    angle = np.float32(2.0 * math.pi) * count / np.float32(NTM * STEPS)
    return np.stack([np.cos(angle), np.sin(angle)]).astype(np.float32)


def shards(depth_class, ocean_mask, depth_levels, drag, tide_force, forward_flow, guess):
    guess = guess[0]
    lat, lat_size = (lax.axis_index("lat"), lax.axis_size("lat"))
    lat = jnp.reshape(lat, (1,)).astype(jnp.int32)
    k = jnp.reshape(lax.axis_index("tm"), (1,)).astype(jnp.int32)
    wave = jnp.asarray(waves())
    block = (ROWS, COLS)
    strip = (8, HALO, COLS)
    side = (ROWS, 256)
    ground, low, high, west, east = call(
        functools.partial(first_kernel, lat_size),
        ((2, *block), strip, strip, side, side),
        [
            pltpu.SMEM((32,), F32),
            pltpu.VMEM(block, jnp.int32),
            pltpu.VMEM(block, jnp.int32),
            pltpu.VMEM(block, F32),
            pltpu.VMEM((2, *block), F32),
            pltpu.VMEM((3, *block), F32),
            pltpu.SemaphoreType.DMA((6,)),
        ],
        [SMEM] + [pl.BlockSpec(memory_space=pltpu.HBM)] * 6,
        60,
    )(lat, depth_levels, depth_class, ocean_mask, drag, tide_force, guess)
    up = [(i, i + 1) for i in range(lat_size - 1)]
    down = [(i + 1, i) for i in range(lat_size - 1)]
    lon_size = lax.axis_size("lon")
    from_west = lax.ppermute(east, "lon", [(i, (i + 1) % lon_size) for i in range(lon_size)])
    from_east = lax.ppermute(west, "lon", [((i + 1) % lon_size, i) for i in range(lon_size)])
    from_south = lax.ppermute(high, "lat", up)
    from_north = lax.ppermute(low, "lat", down)
    fields = (ground, drag, tide_force, guess)
    deep = (3, EROWS, COLS)
    inner_fixed, half, gone = call(
        interior_kernel,
        ((10, EROWS, COLS), deep, deep),
        [pltpu.VMEM((8, EROWS, COLS), F32)],
        [SMEM, SMEM] + [VMEM] * 6,
        8,
        FLOPS,
    )(k, wave, *fields, from_south, from_north)
    from_west, from_east, half = lax.optimization_barrier((from_west, from_east, half))
    (inner,) = call(second_kernel, (deep,), [], [SMEM, SMEM] + [VMEM] * 3, 4, FLOPS)(
        k, wave, inner_fixed, half, gone
    )
    to_north = jnp.concatenate([from_west[ROWS - HALO :], from_east[ROWS - HALO :]])
    to_south = jnp.concatenate([from_west[:HALO], from_east[:HALO]])
    corner_south = lax.ppermute(to_north, "lat", up)
    corner_north = lax.ppermute(to_south, "lat", down)
    sent, fixed, flows = call(
        edge_kernel,
        ((NTM, 3 * CROWS, 128), (10, CROWS, 128), (4, OROWS, 128)),
        [
            pltpu.VMEM((8, EROWS, 128), F32),
            pltpu.VMEM((10, EROWS, 128), F32),
            pltpu.VMEM((3, EROWS, 128), F32),
            pltpu.VMEM((3, EROWS, 128), F32),
        ],
        [SMEM, SMEM] + [VMEM] * 13,
        8,
    )(
        k, wave, *fields, forward_flow, from_south, from_north, from_west, from_east,
        corner_south, corner_north, inner_fixed, inner,
    )
    got = lax.all_to_all(sent, "tm", 0, 0, tiled=True)
    (back,) = call(
        last_kernel,
        ((NTM, OROWS, COLS),),
        [
            pltpu.VMEM((NTM, 3, CROWS, 128), F32),
            pltpu.VMEM((NTM, 3, CROWS, 128), F32),
            pltpu.VMEM((4, CROWS, 128), F32),
        ],
        [SMEM] + [VMEM] * 3,
        10,
    )(wave, got, fixed, flows)
    home = lax.all_to_all(back, "tm", 0, 0, tiled=True)
    state, grad = call(unpack_kernel, ((3, *block), block), [], [VMEM], 6)(home)
    return (state[None], grad)


def solution(mesh):
    return jax.shard_map(
        shards,
        mesh=mesh,
        in_specs=(
            P("lat", "lon"),
            P("lat", "lon"),
            P(),
            P("lat", "lon"),
            P(None, "lat", "lon"),
            P(None, "lat", "lon"),
            P("tm", None, "lat", "lon"),
        ),
        out_specs=(P("tm", None, "lat", "lon"), P("lat", "lon")),
        check_vma=False,
    )
```
